512 devices in a mesh: gs: 128 (over y, z, core), view: 4 (over x).
Axes of the slice: x: 4, y: 8, z: 8, core: 2. Of those that a mesh axis runs over, the one named last changes fastest.
Arguments:
- features: bfloat16 [131072, 128], P('gs'), may hold values from -6 to 6
- geometry: float32 [4, 9, 131072], P('view', None, 'gs'), as said below
- decoder: bfloat16 [128, 512], replicated, may hold values from -0.5 to 0.5
- teacher: bfloat16 [4, 131072, 512], P('view', 'gs'), may hold values from -3 to 3
- images: float32 [4, 3, 131072], P('view', None, 'gs'), may hold values from 0 to 1
- send_index: int32 [4, 128, 1024], P('view', 'gs'), may hold values from 0 to 1023, as said below
- tile_lists: int32 [4, 512, 8], P('view', 'gs'), may hold values from 0 to 7, as said below
- tile_lengths: int32 [4, 512], P('view', 'gs'), may hold values from 2 to 8
Outputs:
- feature_grad: float32 [131072, 128], P(('gs', 'view'))
- geometry_grad: float32 [4, 9, 131072], P('view', None, 'gs')
- decoder_grad: float32 [128, 512], replicated
The draws below stay inside these ranges and needn't reach their ends.
Inputs may be any that keep to these rules, and one draw needn't show every extreme that they name: `send_index`: each row (one view, one source device) is a permutation of 0 .. 1023; positions k * 8 to (k + 1) * 8 - 1 hold the Gaussians sent to the device of gs index k. `tile_lists`: the 8 entries of a row are distinct. `geometry`: opacity logits lie in -7.5 .. -4, log conics between -2 log 16 and -2 log 16 + 2 log 4, shears in -2 .. 2, colors in 0 .. 1.
All inputs are finite; a program needn't handle non-finite values.
Results may differ from the reference program's by a relative error of at most 0.0017.
Values may be sent and summed in bfloat16 or wider, within the bound.
A program may use at most 64 MiB of HBM per device.

```python
import math
import jax
import jax.numpy as jnp
from jax import lax

FEAT = 128
CT = 512
TS = 16
BLK = 128
TILES_DEV = 4
G_DEV = 1024
LIST = 8
SHARDS = 128
VIEWS = 4
G = 131072
TILES = 512
PIX = 131072
N_GS = 128


def sending_order(key):
    scores = jax.random.randint(jax.random.fold_in(key, 11), (VIEWS, SHARDS, G_DEV), 0, 4096) * G_DEV + jnp.arange(G_DEV, dtype=jnp.int32)
    return jnp.argsort(scores, axis=-1).astype(jnp.int32)


def draw_send_index(key, part):
    return sending_order(key)


def draw_geometry(key, part):
    sequence = sending_order(key)
    position = jnp.argsort(sequence, axis=-1).astype(jnp.int32)
    target = (position // (G_DEV // SHARDS)).reshape(VIEWS, SHARDS * G_DEV)
    subkeys = jax.random.split(jax.random.fold_in(key, 37), 7)
    grid_shape = (VIEWS, SHARDS * G_DEV)
    side = float(TS)
    log_low = -2.0 * math.log(side)
    log_high = log_low + 2.0 * math.log(4.0)
    patch_x = (2 * TS * (target % 30)).astype(jnp.float32)
    patch_y = (2 * TS * (target // 30)).astype(jnp.float32)
    center_x = patch_x + jax.random.uniform(subkeys[0], grid_shape, jnp.float32, -0.5 * side, 2.5 * side)
    center_y = patch_y + jax.random.uniform(subkeys[1], grid_shape, jnp.float32, -0.5 * side, 2.5 * side)
    log_a = jax.random.uniform(subkeys[2], grid_shape, jnp.float32, log_low, log_high)
    log_c = jax.random.uniform(subkeys[3], grid_shape, jnp.float32, log_low, log_high)
    shear = jax.random.uniform(subkeys[4], grid_shape, jnp.float32, -2.0, 2.0)
    logit = jax.random.uniform(subkeys[5], grid_shape, jnp.float32, -7.5, -4.0)
    tint = jax.random.uniform(subkeys[6], (VIEWS, 3, SHARDS * G_DEV), jnp.float32, 0.0, 1.0)
    scalars = jnp.stack([center_x, center_y, log_a, log_c, shear, logit], axis=1)
    return jnp.concatenate([scalars, tint], axis=1)


def draw_tile_lists(key, part):
    nblocks = G_DEV // BLK
    scores = jax.random.randint(jax.random.fold_in(key, 23), (VIEWS, SHARDS * TILES_DEV, nblocks), 0, 4096) * nblocks + jnp.arange(nblocks, dtype=jnp.int32)
    return jnp.argsort(scores, axis=-1)[:, :, :LIST].astype(jnp.int32)


def place_ends(entries, stream_key, smallest, top_value):
    spot = [jax.random.randint(jax.random.fold_in(stream_key, axis), (), 0, length) for axis, length in enumerate(entries.shape)]
    widest = entries.shape.index(max(entries.shape))
    neighbour = spot[:widest] + [(spot[widest] + 1) % entries.shape[widest]] + spot[widest + 1:]
    return entries.at[tuple(spot)].set(smallest).at[tuple(neighbour)].set(top_value)


def steps_of(key, shape, shards, least, largest):
    def one(dim, shards_of):
        steps = jax.random.uniform(jax.random.fold_in(jax.random.fold_in(key, 6), dim), (shards_of,), jnp.float32, least / len(shards), largest / len(shards))
        return jnp.repeat(jnp.exp(steps), shape[dim] // shards_of).reshape((-1,) + (1,) * (len(shape) - dim - 1))

    gain = one(*shards[0])
    for cut in shards[1:]:
        gain = gain * one(*cut)
    return gain


def normal_values(stream_key, dims, scale, bound, pieces=(), kind=jnp.bfloat16):
    gain = steps_of(stream_key, dims, pieces, -0.22, 0.18) if pieces else 1.0
    array = jax.random.normal(stream_key, dims, jnp.float32) * scale * gain
    return jnp.minimum(jnp.maximum(array, -bound), bound).astype(kind)


def setup_inputs(seed: int = 0) -> dict:
    streams_of = jax.random.split(jax.random.key(seed), 9)
    return {
        "features": normal_values(streams_of[0], (G, FEAT), 1.0, 6.0, ((0, 128),)),
        "geometry": draw_geometry(jax.random.fold_in(streams_of[8], 71), 0),
        "decoder": normal_values(streams_of[2], (FEAT, CT), FEAT ** -0.5, 0.5),
        "teacher": normal_values(streams_of[3], (VIEWS, PIX, CT), 0.5, 3.0, ((0, 4), (1, 128))),
        "images": jnp.clip(1.0 * jax.random.uniform(streams_of[4], (VIEWS, 3, PIX), jnp.float32) ** steps_of(streams_of[4], (VIEWS, 3, PIX), ((0, 4), (2, 128)), -0.2, 0.2), 0.0, 1.0),
        "send_index": draw_send_index(jax.random.fold_in(streams_of[8], 71), 0),
        "tile_lists": draw_tile_lists(jax.random.fold_in(streams_of[8], 71), 0),
        "tile_lengths": place_ends(jax.random.randint(streams_of[7], (VIEWS, TILES), max(LIST // 4, 1), LIST + 1), jax.random.fold_in(streams_of[7], 1), max(LIST // 4, 1), LIST).astype(jnp.int32),
    }


def composite(tile_geo, alive_mask, pixel_x, pixel_y):
    delta_x = pixel_x[:, None] - tile_geo[0][None, :]
    delta_y = pixel_y[:, None] - tile_geo[1][None, :]
    conic_a = jnp.exp(tile_geo[2])
    conic_c = jnp.exp(tile_geo[3])
    conic_b = 0.8 * jnp.tanh(tile_geo[4]) * jnp.exp(0.5 * (tile_geo[2] + tile_geo[3]))
    exponent = -0.5 * (conic_a * delta_x * delta_x + 2.0 * conic_b * delta_x * delta_y + conic_c * delta_y * delta_y)
    opacity = alive_mask * jax.nn.sigmoid(tile_geo[5])
    alpha_val = opacity[None, :] * jnp.exp(exponent)
    log_keep = jnp.log1p(-alpha_val)
    before = jnp.cumsum(log_keep, axis=1) - log_keep
    weights = alpha_val * jnp.exp(before)
    pixel_color = jnp.einsum('pi,ci->cp', weights, tile_geo[6:9], precision=lax.Precision.HIGHEST)
    return (weights, pixel_color)

def device_terms(recv_geo, recv_feat, decoder, teacher_dev, images_dev, lists, lengths, shard_index):
    nblocks = recv_feat.shape[0] // BLK
    tile_pixels = TS * TS
    geo_blocks = recv_geo.reshape(9, nblocks, BLK)
    feat_blocks = recv_feat.reshape(nblocks, BLK, FEAT)
    within = jnp.arange(tile_pixels, dtype=jnp.int32)
    block_range = jnp.arange(nblocks, dtype=jnp.int32)
    slot_range = jnp.arange(LIST, dtype=jnp.int32)

    def tile_step(totals, tile_index):
        decoder_sum, geo_acc, feat_acc = totals
        block_ids = lists[tile_index]
        count = lengths[tile_index]
        alive_mask = jnp.broadcast_to((slot_range < count).astype(jnp.float32)[:, None], (LIST, BLK)).reshape(LIST * BLK)
        tile_geo = jnp.take(geo_blocks, block_ids, axis=1).reshape(9, LIST * BLK)
        feat_tile = jnp.take(feat_blocks, block_ids, axis=0).reshape(LIST * BLK, FEAT)
        column = 2 * TS * (shard_index % 30) + TS * (tile_index % 2) + within % TS
        row_index = 2 * TS * (shard_index // 30) + TS * (tile_index // 2) + within // TS
        pixel_x = column.astype(jnp.float32) + 0.5
        pixel_y = row_index.astype(jnp.float32) + 0.5
        (weights, pixel_color), pullback = jax.vjp(lambda geo_part: composite(geo_part, alive_mask, pixel_x, pixel_y), tile_geo)
        weight_b = weights.astype(jnp.bfloat16)
        rendered = jnp.dot(weight_b, feat_tile, preferred_element_type=jnp.float32).astype(jnp.bfloat16)
        pred = jnp.dot(rendered, decoder, preferred_element_type=jnp.float32)
        teacher_rows = lax.dynamic_slice_in_dim(teacher_dev, tile_index * tile_pixels, tile_pixels, 0)
        error_feat = pred - teacher_rows.astype(jnp.float32)
        gpred = (error_feat / jnp.sqrt(error_feat * error_feat + 0.04)).astype(jnp.bfloat16)
        grender = lax.dot_general(gpred, decoder, (((1,), (1,)), ((), ())), preferred_element_type=jnp.float32).astype(jnp.bfloat16)
        decoder_sum = decoder_sum + lax.dot_general(rendered, gpred, (((0,), (0,)), ((), ())), preferred_element_type=jnp.float32)
        image_cols = lax.dynamic_slice_in_dim(images_dev, tile_index * tile_pixels, tile_pixels, 1)
        error_color = pixel_color - image_cols
        gcolor = error_color / jnp.sqrt(error_color * error_color + 0.04)
        gweight = lax.dot_general(grender, feat_tile, (((1,), (1,)), ((), ())), preferred_element_type=jnp.float32)
        gfeat_tile = lax.dot_general(weight_b, grender, (((0,), (0,)), ((), ())), preferred_element_type=jnp.float32)
        ggeo_tile, = pullback((gweight, gcolor))
        hits = (block_ids[:, None] == block_range[None, :]).astype(jnp.float32)
        geo_acc = geo_acc + jnp.einsum('clb,ln->cnb', ggeo_tile.reshape(9, LIST, BLK), hits, precision=lax.Precision.HIGHEST)
        feat_acc = feat_acc + jnp.einsum('ln,lbf->nbf', hits, gfeat_tile.reshape(LIST, BLK, FEAT), precision=lax.Precision.HIGHEST)
        return ((decoder_sum, geo_acc, feat_acc), None)
    start_totals = (jnp.zeros((FEAT, CT), jnp.float32), jnp.zeros((9, nblocks, BLK), jnp.float32), jnp.zeros((nblocks, BLK, FEAT), jnp.float32))
    tile_range = jnp.arange(lists.shape[0], dtype=jnp.int32)
    (decoder_sum, geo_acc, feat_acc), _ = lax.scan(tile_step, start_totals, tile_range)
    return (decoder_sum, geo_acc.reshape(9, nblocks * BLK), feat_acc.reshape(nblocks * BLK, FEAT))

def reference(features, geometry, decoder, teacher, images, send_index, tile_lists, tile_lengths):
    slot_size = G_DEV // N_GS
    span = TILES_DEV * TS * TS
    zero_index = jnp.zeros((), jnp.int32)
    source_base = jnp.arange(N_GS, dtype=jnp.int32)[:, None] * G_DEV

    def device_step(totals, flat_index):
        decoder_total, geo_grad, feat_grad = totals
        view_index = flat_index // N_GS
        shard_index = flat_index % N_GS
        send_part = lax.dynamic_slice(send_index, (view_index, zero_index, shard_index * slot_size), (1, N_GS, slot_size))[0]
        recv_ids = (source_base + send_part).reshape(-1).astype(jnp.int32)
        geo_view = lax.dynamic_index_in_dim(geometry, view_index, 0, keepdims=False)
        recv_geo = jnp.take(geo_view, recv_ids, axis=1)
        recv_feat = jnp.take(features, recv_ids, axis=0)
        teacher_dev = lax.dynamic_slice(teacher, (view_index, shard_index * span, zero_index), (1, span, CT))[0]
        images_dev = lax.dynamic_slice(images, (view_index, zero_index, shard_index * span), (1, 3, span))[0]
        lists = lax.dynamic_slice(tile_lists, (view_index, shard_index * TILES_DEV, zero_index), (1, TILES_DEV, LIST))[0]
        lengths = lax.dynamic_slice(tile_lengths, (view_index, shard_index * TILES_DEV), (1, TILES_DEV))[0]
        decoder_sum, geo_acc, feat_acc = device_terms(recv_geo, recv_feat, decoder, teacher_dev, images_dev, lists, lengths, shard_index)
        view_grad = lax.dynamic_index_in_dim(geo_grad, view_index, 0, keepdims=False)
        view_grad = view_grad.at[:, recv_ids].add(geo_acc)
        geo_grad = lax.dynamic_update_index_in_dim(geo_grad, view_grad, view_index, 0)
        feat_grad = feat_grad.at[recv_ids].add(feat_acc)
        return ((decoder_total + decoder_sum, geo_grad, feat_grad), None)
    start_totals = (jnp.zeros((FEAT, CT), jnp.float32), jnp.zeros((VIEWS, 9, G), jnp.float32), jnp.zeros((G, FEAT), jnp.float32))
    flat_range = jnp.arange(VIEWS * N_GS, dtype=jnp.int32)
    (decoder_total, geo_grad, feat_grad), _ = lax.scan(device_step, start_totals, flat_range)
    decoder_grad = decoder_total * (1.0 / math.sqrt(VIEWS * PIX))
    return (feat_grad, geo_grad, decoder_grad)
```

```python
import functools, math
import numpy as np
import jax, jax.numpy as jnp
from jax import lax
from jax.experimental import pallas as pl
from jax.experimental.pallas import tpu as pltpu
from jax.sharding import PartitionSpec as P

FEAT = 128
CT = 512
TS = 16
BLK = 128
LIST = 8
PIX = TS * TS
F32 = jnp.float32
BF16 = jnp.bfloat16
LOG2E = 1.4426950408889634


def pixel_tables(tiles):
    q = np.arange(PIX)
    basis = np.zeros((tiles, 128, PIX), np.float32)
    moments = np.zeros((tiles, PIX, 128), np.float32)
    for k in range(tiles):
        px = TS * (k % 2) + q % TS + 0.5 - TS
        py = TS * (k // 2) + q // TS + 0.5 - TS
        rows = [np.ones(PIX), px, py]
        for square in (px * px, px * py, py * py):
            high = square.astype(jnp.bfloat16).astype(np.float64)
            rows += [high, square - high]
        row = 32
        for index, values in enumerate(rows):
            basis[k, row : row + 3] = values
            row += 3
            moments[k, :, 32 + index] = values
    return basis.astype(jnp.bfloat16), moments.astype(jnp.bfloat16)


def order_tables():
    i = np.arange(BLK)
    before = (i[None, :] < i[:, None]).astype(np.float32)
    after = (i[None, :] > i[:, None]).astype(np.float32)
    return np.stack(
        [np.concatenate([before, before], 1), np.concatenate([after, after], 1)]
    ).astype(jnp.bfloat16)


def pieces(x, count):
    parts = []
    for _ in range(count):
        part = x.astype(BF16)
        parts.append(part)
        x = x - part.astype(F32)
    return parts


def dot(a, b):
    return jnp.dot(a, b, preferred_element_type=F32)


def tiles_kernel(
    lists_ref, lengths_ref, base_ref,
    geo_ref, feat_ref, decoder_ref, teacher_ref, images_ref, basis_ref, moments_ref, order_ref,
    geo_grad_ref, feat_grad_ref, decoder_grad_ref,
    rows, columns, feat_t, alphas, weights, weights_b, terms, right, small,
):
    tile = pl.program_id(0)
    tiles = pl.num_programs(0)
    count = geo_ref.shape[1]
    nblocks = count // BLK

    def parameters():
        x = jnp.clip(geo_ref[0:1, :] - base_ref[0], -4096.0, 4096.0)
        y = jnp.clip(geo_ref[1:2, :] - base_ref[1], -4096.0, 4096.0)
        a = jnp.exp(geo_ref[2:3, :])
        c = jnp.exp(geo_ref[3:4, :])
        slope = jnp.tanh(geo_ref[4:5, :])
        scale = 0.8 * jnp.exp(0.5 * (geo_ref[2:3, :] + geo_ref[3:4, :]))
        return x, y, a, c, slope, scale

    @pl.when(tile == 0)
    def _():
        rows[...] = jnp.zeros_like(rows)
        feat_grad_ref[...] = jnp.zeros_like(feat_grad_ref)
        decoder_grad_ref[...] = jnp.zeros_like(decoder_grad_ref)
        small[...] = jnp.zeros_like(small)
        x, y, a, c, slope, scale = parameters()
        b = slope * scale
        logit = geo_ref[5:6, :]
        log_opacity = -jnp.log(1.0 + jnp.exp(-logit))
        ax_by = a * x + b * y
        bx_cy = b * x + c * y
        constant = log_opacity - 0.5 * (x * ax_by + y * bx_cy)
        row = 32
        for coefficient, repeats in (
            (constant, 1), (ax_by, 1), (bx_cy, 1), (-0.5 * a, 2), (-b, 2), (-0.5 * c, 2)
        ):
            parts = pieces(coefficient * LOG2E, 3)
            for _ in range(repeats):
                for part in parts:
                    rows[row : row + 1, :] = part.astype(F32)
                    row += 1
        high, middle, low = pieces(geo_ref[6:9, :], 3)
        for index, part in enumerate((high, high, middle, high, middle, low)):
            rows[3 * index : 3 * index + 3, :] = part.astype(F32)
        for n in range(nblocks):
            span = slice(n * BLK, (n + 1) * BLK)
            columns[span, 0:BLK] = feat_ref[span, :]
            columns[span, BLK : 2 * BLK] = rows[:, span].T.astype(BF16)
            feat_t[n, 0:FEAT, :] = feat_ref[span, :].astype(F32).T.astype(BF16)
            feat_t[n, FEAT : FEAT + 32, :] = rows[0:32, span].astype(BF16)

    length = lengths_ref[tile]
    ids = [lists_ref[tile, slot] for slot in range(LIST)]
    starts = [pl.multiple_of(block * BLK, BLK) for block in ids]
    before = order_ref[0]
    after = order_ref[1]
    basis = basis_ref[0]

    carry = jnp.zeros((1, PIX), F32)
    acc = jnp.zeros((FEAT + 32, PIX), F32)
    acc_low = jnp.zeros((32, PIX), F32)
    for slot in range(LIST):
        span = slice(slot * BLK, (slot + 1) * BLK)
        exponent = dot(columns[pl.ds(starts[slot], BLK), BLK : 2 * BLK], basis)
        exponent = jnp.where(slot < length, exponent, -1e30)
        alpha = jnp.exp2(exponent)
        log_keep = alpha * (-LOG2E + alpha * (-LOG2E / 2 + alpha * (-LOG2E / 3 + alpha * (-LOG2E / 4))))
        high, low = pieces(log_keep, 2)
        inner = dot(before, jnp.concatenate([high, low], 0))
        weight = alpha * jnp.exp2(inner + carry)
        carry = carry + inner[BLK - 1 : BLK, :] + log_keep[BLK - 1 : BLK, :]
        weight_b, weight_low = pieces(weight, 2)
        alphas[span, :] = alpha
        weights[span, :] = weight
        weights_b[span, 0:PIX] = weight_b
        weights_b[span, PIX : 2 * PIX] = weight_low
        acc = acc + dot(feat_t[ids[slot]], weight_b)
        acc_low = acc_low + dot(feat_t[ids[slot], FEAT : FEAT + 32, :], weight_low)

    rendered_t = acc[0:FEAT, :].astype(BF16)
    color = (
        acc[FEAT : FEAT + 3] + acc[FEAT + 6 : FEAT + 9] + acc[FEAT + 15 : FEAT + 18]
        + acc_low[0:3] + acc_low[6:9]
    )
    error_color = color - images_ref[...]
    gcolor = error_color * lax.rsqrt(error_color * error_color + 0.04)
    rendered = acc[0:FEAT, :].T.astype(BF16)
    pred = dot(rendered, decoder_ref[...])
    error = pred - teacher_ref[...].astype(F32)
    gpred = (error * lax.rsqrt(error * error + 0.04)).astype(BF16)
    decoder_grad_ref[...] += dot(rendered_t, gpred)
    grender_t = lax.dot_general(
        decoder_ref[...], gpred, (((1,), (1,)), ((), ())), preferred_element_type=F32
    )
    terms[0:FEAT, :] = grender_t
    terms[FEAT:, :] = jnp.zeros_like(terms[FEAT:, :])
    high, middle, low = pieces(gcolor, 3)
    for index, part in enumerate((high, middle, high, low, middle, high)):
        terms[FEAT + 3 * index : FEAT + 3 * index + 3, :] = part.astype(F32)
    left = terms[...].astype(BF16)
    right[...] = terms[...].T.astype(BF16)
    moments = moments_ref[0]

    carry = jnp.zeros((1, PIX), F32)
    for slot in reversed(range(LIST)):
        span = slice(slot * BLK, (slot + 1) * BLK)
        gweight = dot(columns[pl.ds(starts[slot], BLK), :], left)
        value = gweight * weights[span, :]
        high, low = pieces(value, 2)
        inner = dot(after, jnp.concatenate([high, low], 0))
        alpha = alphas[span, :]
        square = alpha * alpha
        ratio = alpha + square
        ratio = ratio + ratio * square
        ratio = ratio + ratio * (square * square)
        gexponent = value - ratio * (inner + carry)
        carry = carry + inner[0:1, :] + value[0:1, :]
        high, low = pieces(gexponent, 2)
        wide = dot(weights_b[span, 0:PIX], right[...])
        narrow = dot(weights_b[span, PIX : 2 * PIX], right[:, FEAT : 2 * FEAT])
        narrow = narrow + dot(high, moments) + dot(low, moments)
        where = pl.ds(starts[slot], BLK)
        feat_grad_ref[where, :] += wide[:, 0:FEAT]
        small[where, :] += wide[:, FEAT : 2 * FEAT] + narrow

    @pl.when(tile == tiles - 1)
    def _():
        for n in range(nblocks):
            span = slice(n * BLK, (n + 1) * BLK)
            rows[:, span] = small[span, :].T
        x, y, a, c, slope, scale = parameters()
        b = slope * scale
        s0, sx, sy = (rows[32 + i : 33 + i, :] for i in range(3))
        sxx, sxy, syy = (rows[35 + 2 * i : 36 + 2 * i, :] + rows[36 + 2 * i : 37 + 2 * i, :] for i in range(3))
        ux = sx - x * s0
        uy = sy - y * s0
        dxx = sxx - 2.0 * x * sx + x * x * s0
        dyy = syy - 2.0 * y * sy + y * y * s0
        dxy = sxy - x * sy - y * sx + x * y * s0
        geo_grad_ref[0:1, :] = a * ux + b * uy
        geo_grad_ref[1:2, :] = b * ux + c * uy
        geo_grad_ref[2:3, :] = -0.5 * (a * dxx + b * dxy)
        geo_grad_ref[3:4, :] = -0.5 * (c * dyy + b * dxy)
        geo_grad_ref[4:5, :] = -dxy * scale * (1.0 - slope * slope)
        geo_grad_ref[5:6, :] = s0 / (1.0 + jnp.exp(geo_ref[5:6, :]))
        geo_grad_ref[6:9, :] = rows[0:3, :] + rows[3:6, :] + rows[9:12, :]


def device_terms(recv_geo, recv_feat, decoder, teacher, images, lists, lengths, shard_index):
    tiles = lists.shape[0]
    count = recv_feat.shape[0]
    basis, moments = pixel_tables(tiles)
    base = jnp.stack([2 * TS * (shard_index % 30) + TS, 2 * TS * (shard_index // 30) + TS]).astype(F32)
    smem = pl.BlockSpec(memory_space=pltpu.SMEM)

    def whole(shape):
        return pl.BlockSpec(shape, lambda k: (0,) * len(shape))

    geo, feat, dec = pl.pallas_call(
        tiles_kernel,
        grid=(tiles,),
        in_specs=[
            smem, smem, smem,
            whole((9, count)), whole((count, FEAT)), whole((FEAT, CT)),
            pl.BlockSpec((PIX, CT), lambda k: (k, 0)),
            pl.BlockSpec((3, PIX), lambda k: (0, k)),
            pl.BlockSpec((1, 128, PIX), lambda k: (k, 0, 0)),
            pl.BlockSpec((1, PIX, 128), lambda k: (k, 0, 0)),
            whole((2, BLK, 2 * BLK)),
        ],
        out_specs=[whole((9, count)), whole((count, FEAT)), whole((FEAT, CT))],
        out_shape=[
            jax.ShapeDtypeStruct((9, count), F32),
            jax.ShapeDtypeStruct((count, FEAT), F32),
            jax.ShapeDtypeStruct((FEAT, CT), F32),
        ],
        scratch_shapes=[
            pltpu.VMEM((128, count), F32),
            pltpu.VMEM((count, 2 * BLK), BF16),
            pltpu.VMEM((count // BLK, FEAT + 32, BLK), BF16),
            pltpu.VMEM((LIST * BLK, PIX), F32),
            pltpu.VMEM((LIST * BLK, PIX), F32),
            pltpu.VMEM((LIST * BLK, 2 * PIX), BF16),
            pltpu.VMEM((2 * FEAT, PIX), F32),
            pltpu.VMEM((PIX, 2 * FEAT), BF16),
            pltpu.VMEM((count, 128), F32),
        ],
        compiler_params=pltpu.CompilerParams(dimension_semantics=("arbitrary",)),
        name="tiles",
    )(lists, lengths, base, recv_geo, recv_feat, decoder, teacher, images,
      jnp.asarray(basis), jnp.asarray(moments), jnp.asarray(order_tables()))
    return dec, geo, feat


def on_device(features, geometry, decoder, teacher, images, send_index, tile_lists, tile_lengths):
    send_order = send_index[0, 0]
    shard_index = lax.axis_index("gs")
    geo_send = jnp.take(geometry[0], send_order, axis=1)
    recv_geo = lax.all_to_all(geo_send, "gs", split_axis=1, concat_axis=1, tiled=True)
    feat_send = jnp.take(features, send_order, axis=0)
    recv_feat = lax.all_to_all(feat_send, "gs", split_axis=0, concat_axis=0, tiled=True)
    decoder_sum, geo_acc, feat_acc = device_terms(
        recv_geo, recv_feat, decoder, teacher[0], images[0], tile_lists[0], tile_lengths[0], shard_index
    )
    returned_geo = lax.all_to_all(geo_acc, "gs", split_axis=1, concat_axis=1, tiled=True)
    returned_feat = lax.all_to_all(feat_acc, "gs", split_axis=0, concat_axis=0, tiled=True)
    geo_own = jnp.zeros_like(returned_geo).at[:, send_order].set(returned_geo)
    feat_own = jnp.zeros_like(returned_feat).at[send_order].set(returned_feat)
    feature_grad = lax.psum_scatter(feat_own, "view", scatter_dimension=0, tiled=True)
    pixel_total = lax.axis_size("gs") * lax.axis_size("view") * tile_lists.shape[1] * PIX
    decoder_grad = lax.psum(decoder_sum, ("gs", "view")) * (1.0 / math.sqrt(pixel_total))
    return (feature_grad, geo_own[None], decoder_grad)


def solution(mesh):
    placed = (
        P("gs", None),
        P("view", None, "gs"),
        P(),
        P("view", "gs", None),
        P("view", None, "gs"),
        P("view", "gs", None),
        P("view", "gs", None),
        P("view", "gs"),
    )
    return jax.shard_map(
        on_device,
        mesh=mesh,
        in_specs=placed,
        out_specs=(P(("gs", "view"), None), P("view", None, "gs"), P()),
        check_vma=False,
    )
```

```python
import functools, math
import numpy as np
import jax, jax.numpy as jnp
from jax import lax
from jax.experimental import pallas as pl
from jax.experimental.pallas import tpu as pltpu
from jax.sharding import PartitionSpec as P

FEAT = 128
CT = 512
TS = 16
BLK = 128
LIST = 8
PIX = TS * TS
F32 = jnp.float32
BF16 = jnp.bfloat16
LOG2E = 1.4426950408889634
SEND = 8


def pixel_tables(tiles):
    q = np.arange(PIX)
    basis = np.zeros((tiles, 128, PIX), np.float32)
    moments = np.zeros((tiles, PIX, 128), np.float32)
    for k in range(tiles):
        px = TS * (k % 2) + q % TS + 0.5 - TS
        py = TS * (k // 2) + q // TS + 0.5 - TS
        rows = [np.ones(PIX), px, py]
        for square in (px * px, px * py, py * py):
            high = square.astype(jnp.bfloat16).astype(np.float64)
            rows += [high, square - high]
        row = 32
        for index, values in enumerate(rows):
            basis[k, row : row + 3] = values
            row += 3
            moments[k, :, 32 + index] = values
    return basis.astype(jnp.bfloat16), moments.astype(jnp.bfloat16)


def order_tables():
    i = np.arange(BLK)
    before = (i[None, :] < i[:, None]).astype(np.float32)
    after = (i[None, :] > i[:, None]).astype(np.float32)
    return np.stack(
        [np.concatenate([before, before], 1), np.concatenate([after, after], 1)]
    ).astype(jnp.bfloat16)


def pieces(x, count):
    parts = []
    for _ in range(count):
        part = x.astype(BF16)
        parts.append(part)
        x = x - part.astype(F32)
    return parts


def dot(a, b):
    return jnp.dot(a, b, preferred_element_type=F32)

def selection(count):
    row = lax.broadcasted_iota(jnp.int32, (128, count), 0)
    column = lax.broadcasted_iota(jnp.int32, (128, count), 1)
    select = jnp.where(row == column // SEND, 1.0, 0.0).astype(BF16)
    return select, row // 16 == column % SEND


def to_rows(parts, select, mask):
    total = None
    for part in parts:
        tiled = jnp.where(mask, jnp.concatenate([part.astype(F32)] * SEND, 0), 0.0).astype(BF16)
        term = lax.dot_general(select, tiled, (((1,), (1,)), ((), ())), preferred_element_type=F32)
        total = term if total is None else total + term
    return total


def from_rows(x, select, mask):
    total = sum(dot(part, select) for part in pieces(x.T, 3))
    total = jnp.where(mask, total, 0.0)
    return sum(total[16 * p : 16 * p + 16, :] for p in range(SEND))


def tiles_kernel(
    lists_ref, lengths_ref, base_ref,
    geo_rows_ref, feat_ref, decoder_ref, teacher_ref, images_ref, basis_ref, moments_ref, order_ref,
    geo_grad_rows_ref, feat_grad_ref, decoder_tiles_ref,
    geo_ref, geo_grad_ref, decoder_grad_ref, rows, columns, feat_t, alphas, weights, weights_b, terms, right, small,
):
    tile = pl.program_id(0)
    tiles = pl.num_programs(0)
    count = feat_ref.shape[0]
    nblocks = count // BLK

    def parameters():
        x = jnp.clip(geo_ref[0:1, :] - base_ref[0], -4096.0, 4096.0)
        y = jnp.clip(geo_ref[1:2, :] - base_ref[1], -4096.0, 4096.0)
        a = jnp.exp(geo_ref[2:3, :])
        c = jnp.exp(geo_ref[3:4, :])
        slope = jnp.tanh(geo_ref[4:5, :])
        scale = 0.8 * jnp.exp(0.5 * (geo_ref[2:3, :] + geo_ref[3:4, :]))
        return x, y, a, c, slope, scale

    @pl.when(tile == 0)
    def _():
        geo_ref[...] = from_rows(geo_rows_ref[...], *selection(count))
        rows[...] = jnp.zeros_like(rows)
        feat_grad_ref[...] = jnp.zeros_like(feat_grad_ref)
        decoder_grad_ref[...] = jnp.zeros_like(decoder_grad_ref)
        small[...] = jnp.zeros_like(small)
        x, y, a, c, slope, scale = parameters()
        b = slope * scale
        logit = geo_ref[5:6, :]
        log_opacity = -jnp.log(1.0 + jnp.exp(-logit))
        ax_by = a * x + b * y
        bx_cy = b * x + c * y
        constant = log_opacity - 0.5 * (x * ax_by + y * bx_cy)
        row = 32
        for coefficient, repeats in (
            (constant, 1), (ax_by, 1), (bx_cy, 1), (-0.5 * a, 2), (-b, 2), (-0.5 * c, 2)
        ):
            parts = pieces(coefficient * LOG2E, 3)
            for _ in range(repeats):
                for part in parts:
                    rows[row : row + 1, :] = part.astype(F32)
                    row += 1
        high, middle, low = pieces(geo_ref[6:9, :], 3)
        for index, part in enumerate((high, high, middle, high, middle, low)):
            rows[3 * index : 3 * index + 3, :] = part.astype(F32)
        for n in range(nblocks):
            span = slice(n * BLK, (n + 1) * BLK)
            columns[span, 0:BLK] = feat_ref[span, :]
            columns[span, BLK : 2 * BLK] = rows[:, span].T.astype(BF16)
            feat_t[n, 0:FEAT, :] = feat_ref[span, :].astype(F32).T.astype(BF16)
            feat_t[n, FEAT : FEAT + 32, :] = rows[0:32, span].astype(BF16)

    length = lengths_ref[tile]
    ids = [lists_ref[tile, slot] for slot in range(LIST)]
    starts = [pl.multiple_of(block * BLK, BLK) for block in ids]
    before = order_ref[0]
    after = order_ref[1]
    basis = basis_ref[0]

    carry = jnp.zeros((1, PIX), F32)
    acc = jnp.zeros((FEAT + 32, PIX), F32)
    acc_low = jnp.zeros((32, PIX), F32)
    for slot in range(LIST):
        span = slice(slot * BLK, (slot + 1) * BLK)
        exponent = dot(columns[pl.ds(starts[slot], BLK), BLK : 2 * BLK], basis)
        exponent = jnp.where(slot < length, exponent, -1e30)
        alpha = jnp.exp2(exponent)
        log_keep = alpha * (-LOG2E + alpha * (-LOG2E / 2 + alpha * (-LOG2E / 3 + alpha * (-LOG2E / 4))))
        high, low = pieces(log_keep, 2)
        inner = dot(before, jnp.concatenate([high, low], 0))
        weight = alpha * jnp.exp2(inner + carry)
        carry = carry + inner[BLK - 1 : BLK, :] + log_keep[BLK - 1 : BLK, :]
        weight_b, weight_low = pieces(weight, 2)
        alphas[span, :] = alpha
        weights[span, :] = weight
        weights_b[span, 0:PIX] = weight_b
        weights_b[span, PIX : 2 * PIX] = weight_low
        acc = acc + dot(feat_t[ids[slot]], weight_b)
        acc_low = acc_low + dot(feat_t[ids[slot], FEAT : FEAT + 32, :], weight_low)

    rendered_t = acc[0:FEAT, :].astype(BF16)
    color = (
        acc[FEAT : FEAT + 3] + acc[FEAT + 6 : FEAT + 9] + acc[FEAT + 15 : FEAT + 18]
        + acc_low[0:3] + acc_low[6:9]
    )
    error_color = color - images_ref[...]
    gcolor = error_color * lax.rsqrt(error_color * error_color + 0.04)
    rendered = acc[0:FEAT, :].T.astype(BF16)
    pred = dot(rendered, decoder_ref[...])
    error = pred - teacher_ref[...].astype(F32)
    gpred = (error * lax.rsqrt(error * error + 0.04)).astype(BF16)
    decoder_grad_ref[...] += dot(rendered_t, gpred)
    grender_t = lax.dot_general(
        decoder_ref[...], gpred, (((1,), (1,)), ((), ())), preferred_element_type=F32
    )
    terms[0:FEAT, :] = grender_t
    terms[FEAT:, :] = jnp.zeros_like(terms[FEAT:, :])
    high, middle, low = pieces(gcolor, 3)
    for index, part in enumerate((high, middle, high, low, middle, high)):
        terms[FEAT + 3 * index : FEAT + 3 * index + 3, :] = part.astype(F32)
    left = terms[...].astype(BF16)
    right[...] = terms[...].T.astype(BF16)
    moments = moments_ref[0]

    carry = jnp.zeros((1, PIX), F32)
    for slot in reversed(range(LIST)):
        span = slice(slot * BLK, (slot + 1) * BLK)
        gweight = dot(columns[pl.ds(starts[slot], BLK), :], left)
        value = gweight * weights[span, :]
        high, low = pieces(value, 2)
        inner = dot(after, jnp.concatenate([high, low], 0))
        alpha = alphas[span, :]
        square = alpha * alpha
        ratio = alpha + square
        ratio = ratio + ratio * square
        ratio = ratio + ratio * (square * square)
        gexponent = value - ratio * (inner + carry)
        carry = carry + inner[0:1, :] + value[0:1, :]
        high, low = pieces(gexponent, 2)
        wide = dot(weights_b[span, 0:PIX], right[...])
        narrow = dot(weights_b[span, PIX : 2 * PIX], right[:, FEAT : 2 * FEAT])
        narrow = narrow + dot(high, moments) + dot(low, moments)
        where = pl.ds(starts[slot], BLK)
        feat_grad_ref[where, :] += wide[:, 0:FEAT]
        small[where, :] += wide[:, FEAT : 2 * FEAT] + narrow

    @pl.when(tile == tiles - 1)
    def _():
        for n in range(nblocks):
            span = slice(n * BLK, (n + 1) * BLK)
            rows[:, span] = small[span, :].T
        x, y, a, c, slope, scale = parameters()
        b = slope * scale
        s0, sx, sy = (rows[32 + i : 33 + i, :] for i in range(3))
        sxx, sxy, syy = (rows[35 + 2 * i : 36 + 2 * i, :] + rows[36 + 2 * i : 37 + 2 * i, :] for i in range(3))
        ux = sx - x * s0
        uy = sy - y * s0
        dxx = sxx - 2.0 * x * sx + x * x * s0
        dyy = syy - 2.0 * y * sy + y * y * s0
        dxy = sxy - x * sy - y * sx + x * y * s0
        geo_grad_ref[0:1, :] = a * ux + b * uy
        geo_grad_ref[1:2, :] = b * ux + c * uy
        geo_grad_ref[2:3, :] = -0.5 * (a * dxx + b * dxy)
        geo_grad_ref[3:4, :] = -0.5 * (c * dyy + b * dxy)
        geo_grad_ref[4:5, :] = -dxy * scale * (1.0 - slope * slope)
        geo_grad_ref[5:6, :] = s0 / (1.0 + jnp.exp(geo_ref[5:6, :]))
        geo_grad_ref[6:9, :] = rows[0:3, :] + rows[3:6, :] + rows[9:12, :]
        geo_grad_ref[9:16, :] = jnp.zeros((7, count), F32)
        geo_grad_rows_ref[...] = to_rows(pieces(geo_grad_ref[...], 3), *selection(count))
        for row in range(FEAT // 8):
            for lane in range(CT // 128):
                decoder_tiles_ref[row * (CT // 128) + lane] = decoder_grad_ref[
                    8 * row : 8 * row + 8, 128 * lane : 128 * lane + 128
                ]


def device_terms(recv_geo, recv_feat, decoder, teacher, images, lists, lengths, shard_index):
    tiles = lists.shape[0]
    count = recv_feat.shape[0]
    basis, moments = pixel_tables(tiles)
    base = jnp.stack([2 * TS * (shard_index % 30) + TS, 2 * TS * (shard_index // 30) + TS]).astype(F32)
    smem = pl.BlockSpec(memory_space=pltpu.SMEM)

    def whole(shape):
        return pl.BlockSpec(shape, lambda k: (0,) * len(shape))

    geo, feat, dec = pl.pallas_call(
        tiles_kernel,
        grid=(tiles,),
        in_specs=[
            smem, smem, smem,
            whole((128, 128)), whole((count, FEAT)), whole((FEAT, CT)),
            pl.BlockSpec((PIX, CT), lambda k: (k, 0)),
            pl.BlockSpec((3, PIX), lambda k: (0, k)),
            pl.BlockSpec((1, 128, PIX), lambda k: (k, 0, 0)),
            pl.BlockSpec((1, PIX, 128), lambda k: (k, 0, 0)),
            whole((2, BLK, 2 * BLK)),
        ],
        out_specs=[whole((128, 128)), whole((count, FEAT)), whole((FEAT * CT // 1024, 8, 128))],
        out_shape=[
            jax.ShapeDtypeStruct((128, 128), F32),
            jax.ShapeDtypeStruct((count, FEAT), F32),
            jax.ShapeDtypeStruct((FEAT * CT // 1024, 8, 128), F32),
        ],
        scratch_shapes=[
            pltpu.VMEM((16, count), F32),
            pltpu.VMEM((16, count), F32),
            pltpu.VMEM((FEAT, CT), F32),
            pltpu.VMEM((128, count), F32),
            pltpu.VMEM((count, 2 * BLK), BF16),
            pltpu.VMEM((count // BLK, FEAT + 32, BLK), BF16),
            pltpu.VMEM((LIST * BLK, PIX), F32),
            pltpu.VMEM((LIST * BLK, PIX), F32),
            pltpu.VMEM((LIST * BLK, 2 * PIX), BF16),
            pltpu.VMEM((2 * FEAT, PIX), F32),
            pltpu.VMEM((PIX, 2 * FEAT), BF16),
            pltpu.VMEM((count, 128), F32),
        ],
        compiler_params=pltpu.CompilerParams(dimension_semantics=("arbitrary",)),
        name="tiles",
    )(lists, lengths, base, recv_geo, recv_feat, decoder, teacher, images,
      jnp.asarray(basis), jnp.asarray(moments), jnp.asarray(order_tables()))
    return dec, geo, feat


Y, Z, C, X = 8, 8, 2, 4
GROUP = (Y, Z, C)


def place():
    index = lax.axis_index("gs")
    return index // (Z * C), (index // C) % Z, index % C, lax.axis_index("view")


def gs_of(y, z, c):
    return (y * Z + z) * C + c


def loop(start, stop, body):
    def step(i, carry):
        body(i)
        return carry

    lax.fori_loop(start, stop, step, 0)


def greet(targets):
    barrier = pltpu.get_barrier_semaphore()
    for count, target in targets:
        loop(0, count, lambda i: pl.semaphore_signal(
            barrier, inc=1, device_id=target(i), device_id_type=pl.DeviceIdType.MESH))
    pl.semaphore_wait(barrier, sum(count for count, _ in targets))


def line_targets():
    y, z, c, _ = place()
    return [
        (Y - 1, lambda i: {"gs": gs_of((y + 1 + i) % Y, z, c)}),
        (Z - 1, lambda i: {"gs": gs_of(y, (z + 1 + i) % Z, c)}),
        (Z, lambda i: {"gs": gs_of(y, i, 1 - c)}),
    ]


def remote(src, dst, sems, mine, theirs, target):
    return pltpu.make_async_remote_copy(
        src_ref=src, dst_ref=dst, send_sem=sems.at[0, mine], recv_sem=sems.at[1, theirs],
        device_id=target, device_id_type=pl.DeviceIdType.MESH,
    )


class Exchange:
    def __init__(self, pairs, sems):
        self.pairs = pairs
        self.sems = sems

    def copies(self, stage, i):
        y, z, c, _ = place()
        out = []
        for n, (send, hop_a, hop_b, recv) in enumerate(self.pairs):
            sems = self.sems.at[4 * n + stage]
            if stage == 0:
                to = (y + i) % Y
                out.append(remote(send.at[to, :, c], hop_a.at[y], sems, i, i, {"gs": gs_of(to, z, c)}))
            elif stage == 1:
                to = (z + i) % Z
                out.append(remote(send.at[:, to, 1 - c], hop_b.at[z], sems, i, i, {"gs": gs_of(y, to, 1 - c)}))
            elif stage == 2:
                to = (z + i) % Z
                out.append(remote(hop_a.at[:, to], recv.at[:, z, c], sems, i, i, {"gs": gs_of(y, to, c)}))
            else:
                to = (y + i) % Y
                out.append(remote(hop_b.at[:, to], recv.at[y, :, 1 - c], sems, i, i, {"gs": gs_of(to, z, c)}))
        return out

    def first(self, stage):
        return 0 if stage == 1 else 1

    def start(self, stage):
        def body(i):
            for copy in self.copies(stage, i):
                copy.start()

        loop(self.first(stage), 8, body)

    def arrive(self, stage):
        def body(i):
            for copy in self.copies(stage, i):
                copy.wait_recv()

        loop(self.first(stage), 8, body)

    def sent(self, stage):
        def body(i):
            for copy in self.copies(stage, i):
                copy.wait_send()

        loop(self.first(stage), 8, body)

    def keep_first(self):
        y, z, c, _ = place()
        for send, hop_a, hop_b, recv in self.pairs:
            hop_a[y] = send[y, :, c]

    def keep_a(self):
        y, z, c, _ = place()
        for send, hop_a, hop_b, recv in self.pairs:
            recv[:, z, c] = hop_a[:, z]

    def keep_b(self):
        y, z, c, _ = place()
        for send, hop_a, hop_b, recv in self.pairs:
            recv[y, :, 1 - c] = hop_b[:, y]


def forward_kernel(
    order_ref, feat_ref, geo_ref, feat_out, geo_out,
    source, gathered, send_f, send_g, a_f, a_g, b_f, b_g, sems,
):
    count = feat_ref.shape[0]
    greet(line_targets())
    for n in range(count // BLK):
        span = slice(n * BLK, (n + 1) * BLK)
        source[0:FEAT, span] = feat_ref[span, :].astype(F32).T.astype(BF16)
    padded = jnp.concatenate([geo_ref[...], jnp.zeros((7, count), F32)], 0)
    for index, part in enumerate(pieces(padded, 3)):
        source[FEAT + 16 * index : FEAT + 16 * index + 16, :] = part
    step = 256
    for n in range(count // step):
        span = slice(n * step, (n + 1) * step)
        row = lax.broadcasted_iota(jnp.int32, (count, step), 0)
        onehot = jnp.where(row == order_ref[:, span], 1.0, 0.0).astype(BF16)
        picked = dot(source[...], onehot)
        block = picked[0:FEAT, :].T.reshape(step // (Z * C * SEND), Z, C, SEND, FEAT).astype(BF16)
        send_f[n * 2 : n * 2 + 2] = block
        gathered[:, span] = picked[FEAT : FEAT + 48, :]
    parts = [gathered[16 * i : 16 * i + 16, :] for i in range(3)]
    rows = to_rows(parts, *selection(count))
    for d in range(Y * Z * C):
        send_g[d // (Z * C), (d // C) % Z, d % C] = rows[d : d + 1, :]

    exchange = Exchange([(send_f, a_f, b_f, feat_out), (send_g, a_g, b_g, geo_out)], sems)
    exchange.start(0)
    exchange.start(1)
    exchange.keep_first()
    exchange.arrive(0)
    exchange.start(2)
    exchange.keep_a()
    exchange.arrive(1)
    exchange.start(3)
    exchange.keep_b()
    exchange.arrive(2)
    exchange.arrive(3)
    for stage in range(4):
        exchange.sent(stage)


def exchange_buffers(dtype):
    return [
        pltpu.VMEM((Y, Z, SEND, FEAT), dtype), pltpu.VMEM((Y, Z, 1, 128), F32),
        pltpu.VMEM((Z, Y, SEND, FEAT), dtype), pltpu.VMEM((Z, Y, 1, 128), F32),
    ]


def forward_exchange(order, features, geometry):
    count = features.shape[0]
    vmem = pl.BlockSpec(memory_space=pltpu.VMEM)
    return pl.pallas_call(
        forward_kernel,
        in_specs=[vmem] * 3,
        out_specs=[vmem] * 2,
        out_shape=[
            jax.ShapeDtypeStruct((*GROUP, SEND, FEAT), BF16),
            jax.ShapeDtypeStruct((*GROUP, 1, 128), F32),
        ],
        scratch_shapes=[
            pltpu.VMEM((FEAT + 48, count), BF16),
            pltpu.VMEM((48, count), F32),
            pltpu.VMEM((*GROUP, SEND, FEAT), BF16),
            pltpu.VMEM((*GROUP, 1, 128), F32),
            *exchange_buffers(BF16),
            pltpu.SemaphoreType.DMA((8, 2, 8)),
        ],
        compiler_params=pltpu.CompilerParams(collective_id=0, has_side_effects=True),
        name="forward_exchange",
    )(order, features, geometry)


def return_kernel(
    scale, order_ref, send_f, send_g, dec_ref, feat_out, geo_out, dec_out,
    a_f, a_g, b_f, b_g, recv_f, recv_g, geo_rows, returned, shares, view_in,
    d1, p1, d2, p2, d3, p3, d4, d5, sems, sum_sems, view_sems,
):
    y, z, c, x = place()
    count = order_ref.shape[1]
    corner = x * C + c

    def xc(i):
        to = (corner + i) % (X * C)
        return to, {"gs": gs_of(y, z, to % C), "view": to // C}

    greet(line_targets() + [
        (X - 1, lambda i: {"gs": gs_of(y, z, c), "view": (x + 1 + i) % X}),
        (X - 1, lambda i: {"gs": gs_of(y, z, 1 - c), "view": (x + 1 + i) % X}),
    ])

    def sum_copy(stage, i):
        sems = sum_sems.at[stage]
        if stage == 0:
            to, target = xc(i)
            return remote(dec_ref.at[pl.ds(to * Z, Z)], d1.at[corner], sems, i, i, target)
        if stage == 1:
            to = (z + i) % Z
            return remote(p1.at[to], d2.at[z], sems, i, i, {"gs": gs_of(y, to, c)})
        if stage == 2:
            to = (y + i) % Y
            return remote(p2, d3.at[y], sems, i, i, {"gs": gs_of(to, z, c)})
        if stage == 3:
            to = (z + i) % Z
            return remote(p3, d4.at[z], sems, i, i, {"gs": gs_of(y, to, c)})
        to, target = xc(i)
        return remote(d4, d5.at[corner], sems, i, i, target)

    def sum_start(stage):
        loop(1, 8, lambda i: sum_copy(stage, i).start())

    def sum_arrive(stage):
        loop(1, 8, lambda i: sum_copy(stage, i).wait_recv())

    exchange = Exchange([(send_f, a_f, b_f, recv_f), (send_g, a_g, b_g, recv_g)], sems)
    sum_start(0)
    exchange.start(0)
    exchange.start(1)
    exchange.keep_first()
    d1[corner] = dec_ref[pl.ds(corner * Z, Z)]
    sum_arrive(0)
    p1[...] = sum(d1[i] for i in range(X * C))
    sum_start(1)
    d2[z] = p1[z]
    sum_arrive(1)
    p2[...] = sum(d2[i] for i in range(Z))
    sum_start(2)
    d3[y] = p2[...]
    exchange.arrive(0)
    exchange.start(2)
    exchange.keep_a()
    exchange.arrive(1)
    exchange.start(3)
    exchange.keep_b()
    sum_arrive(2)
    p3[...] = sum(d3[i] for i in range(Y)) * scale
    sum_start(3)
    d4[z] = p3[...]
    sum_arrive(3)
    sum_start(4)
    d5[corner] = d4[...]
    exchange.arrive(2)
    exchange.arrive(3)

    for d in range(Y * Z * C):
        geo_rows[d : d + 1, :] = recv_g[d // (Z * C), (d // C) % Z, d % C]
    geo = from_rows(geo_rows[...], *selection(count))
    geo_parts = jnp.concatenate([part.astype(F32) for part in pieces(geo, 3)], 0).astype(BF16)
    for n in range(Y):
        high, low = pieces(recv_f[n].reshape(Z * C * SEND, FEAT), 2)
        span = slice(n * Z * C * SEND, (n + 1) * Z * C * SEND)
        returned[span, 0:FEAT] = high
        returned[span, FEAT : 2 * FEAT] = low

    quarter = count // X

    def view_copy(i):
        return remote(
            shares.at[i], view_in.at[x], view_sems, i, i, {"gs": gs_of(y, z, c), "view": (x + i) % X}
        )

    for i in (1, 2, 3, 0):
        start = pl.multiple_of(((x + i) % X) * quarter, quarter)
        row = lax.broadcasted_iota(jnp.int32, (quarter, count), 0) + start
        onehot = jnp.where(row == order_ref[...], 1.0, 0.0).astype(BF16)
        both = dot(onehot, returned[...])
        share = both[:, 0:FEAT] + both[:, FEAT : 2 * FEAT]
        if i:
            shares[i] = share
            view_copy(i).start()
        else:
            view_in[x] = share
        own = lax.dot_general(geo_parts, onehot, (((1,), (1,)), ((), ())), preferred_element_type=F32)
        own = own[0:16] + own[16:32] + own[32:48]
        geo_out[:, pl.ds(start, quarter)] = own[0:9]

    sum_arrive(4)
    for row in range(FEAT // 8):
        for lane in range(CT // 128):
            n = row * (CT // 128) + lane
            dec_out[8 * row : 8 * row + 8, 128 * lane : 128 * lane + 128] = d5[n // Z, n % Z]
    for i in (1, 2, 3):
        view_copy(i).wait_recv()
    feat_out[...] = view_in[0] + view_in[1] + view_in[2] + view_in[3]
    for i in (1, 2, 3):
        view_copy(i).wait_send()
    for stage in range(5):
        loop(1, 8, lambda i: sum_copy(stage, i).wait_send())
    for stage in range(4):
        exchange.sent(stage)


def return_exchange(order, feat, geo, dec, scale):
    count = order.shape[1]
    quarter = count // X
    vmem = pl.BlockSpec(memory_space=pltpu.VMEM)
    tile = (8, 128)
    return pl.pallas_call(
        functools.partial(return_kernel, scale),
        in_specs=[vmem] * 4,
        out_specs=[vmem] * 3,
        out_shape=[
            jax.ShapeDtypeStruct((quarter, FEAT), F32),
            jax.ShapeDtypeStruct((9, count), F32),
            jax.ShapeDtypeStruct((FEAT, CT), F32),
        ],
        scratch_shapes=[
            *exchange_buffers(F32),
            pltpu.VMEM((*GROUP, SEND, FEAT), F32),
            pltpu.VMEM((*GROUP, 1, 128), F32),
            pltpu.VMEM((128, 128), F32),
            pltpu.VMEM((count, 2 * FEAT), BF16),
            pltpu.VMEM((X, quarter, FEAT), F32),
            pltpu.VMEM((X, quarter, FEAT), F32),
            pltpu.VMEM((X * C, Z, *tile), F32),
            pltpu.VMEM((Z, *tile), F32),
            pltpu.VMEM((Z, *tile), F32),
            pltpu.VMEM(tile, F32),
            pltpu.VMEM((Y, *tile), F32),
            pltpu.VMEM(tile, F32),
            pltpu.VMEM((Z, *tile), F32),
            pltpu.VMEM((X * C, Z, *tile), F32),
            pltpu.SemaphoreType.DMA((8, 2, 8)),
            pltpu.SemaphoreType.DMA((5, 2, 8)),
            pltpu.SemaphoreType.DMA((2, X)),
        ],
        compiler_params=pltpu.CompilerParams(collective_id=1, has_side_effects=True),
        name="return_exchange",
    )(order, feat, geo, dec)


def on_device(features, geometry, decoder, teacher, images, send_index, tile_lists, tile_lengths):
    order = send_index[0]
    shard_index = lax.axis_index("gs")
    recv_feat, recv_geo = forward_exchange(order, features, geometry[0])
    pixel_total = lax.axis_size("gs") * lax.axis_size("view") * tile_lists.shape[1] * PIX
    dec, geo, feat = device_terms(
        recv_geo.reshape(128, 128), recv_feat.reshape(-1, FEAT), decoder, teacher[0], images[0],
        tile_lists[0], tile_lengths[0], shard_index,
    )
    feature_grad, geo_own, decoder_grad = return_exchange(
        order, feat.reshape(*GROUP, SEND, FEAT), geo.reshape(*GROUP, 1, 128), dec, 1.0 / math.sqrt(pixel_total)
    )
    return (feature_grad, geo_own[None], decoder_grad)


def solution(mesh):
    placed = (
        P("gs", None),
        P("view", None, "gs"),
        P(),
        P("view", "gs", None),
        P("view", None, "gs"),
        P("view", "gs", None),
        P("view", "gs", None),
        P("view", "gs"),
    )
    return jax.shard_map(
        on_device,
        mesh=mesh,
        in_specs=placed,
        out_specs=(P(("gs", "view"), None), P("view", None, "gs"), P()),
        check_vma=False,
    )
```

```python
import functools
import math

import jax
import jax.numpy as jnp
import numpy as np
from jax import lax
from jax.experimental import pallas as pl
from jax.experimental.pallas import tpu as pltpu
from jax.sharding import PartitionSpec as P

FEAT = 128
CT = 512
TS = 16
BLK = 128
LIST = 8
PIX = TS * TS
SEND = 8
Y, Z, C, X = 8, 8, 2, 4
GROUP = (Y, Z, C)
F32 = jnp.float32
BF16 = jnp.bfloat16
LOG2E = 1.4426950408889634


def pixel_tables(tiles):
    q = np.arange(PIX)
    basis = np.zeros((tiles, 128, PIX), np.float32)
    moments = np.zeros((tiles, PIX, 128), np.float32)
    for k in range(tiles):
        px = TS * (k % 2) + q % TS + 0.5 - TS
        py = TS * (k // 2) + q // TS + 0.5 - TS
        rows = [np.ones(PIX), px, py]
        for square in (px * px, px * py, py * py):
            high = square.astype(jnp.bfloat16).astype(np.float64)
            rows += [high, square - high]
        row = 32
        for index, values in enumerate(rows):
            basis[k, row : row + 3] = values
            row += 3
            moments[k, :, 32 + index] = values
    return basis.astype(jnp.bfloat16), moments.astype(jnp.bfloat16)


def order_tables():
    i = np.arange(BLK)
    before = (i[None, :] < i[:, None]).astype(np.float32)
    after = (i[None, :] > i[:, None]).astype(np.float32)
    return np.stack(
        [np.concatenate([before, before], 1), np.concatenate([after, after], 1)]
    ).astype(jnp.bfloat16)


def pieces(x, count):
    parts = []
    for _ in range(count):
        part = x.astype(BF16)
        parts.append(part)
        x = x - part.astype(F32)
    return parts


def dot(a, b):
    return jnp.dot(a, b, preferred_element_type=F32)


def dot_t(a, b):
    return lax.dot_general(a, b, (((1,), (1,)), ((), ())), preferred_element_type=F32)


def to_rows(parts, select, mask):
    total = None
    for part in parts:
        tiled = (jnp.concatenate([part.astype(F32)] * SEND, 0) * mask).astype(BF16)
        term = dot_t(select, tiled)
        total = term if total is None else total + term
    return total


def from_rows(x, select, mask):
    total = sum(dot(part, select) for part in pieces(x.T, 3)) * mask
    return sum(total[16 * p : 16 * p + 16, :] for p in range(SEND))


def place():
    index = lax.axis_index("gs")
    return index // (Z * C), (index // C) % Z, index % C, lax.axis_index("view")


def gs_of(y, z, c):
    return (y * Z + z) * C + c


def loop(start, stop, body):
    def step(i, carry):
        body(i)
        return carry

    lax.fori_loop(start, stop, step, 0)


def remote(src, dst, sems, i, target):
    return pltpu.make_async_remote_copy(
        src_ref=src, dst_ref=dst, send_sem=sems.at[0, i], recv_sem=sems.at[1, i],
        device_id=target, device_id_type=pl.DeviceIdType.MESH,
    )


class Exchange:
    def __init__(self, pairs, sems):
        self.pairs = pairs
        self.sems = sems

    def copies(self, stage, i):
        y, z, c, _ = place()
        out = []
        for n, (send, hop_a, hop_b, recv) in enumerate(self.pairs):
            sems = self.sems.at[4 * n + stage]
            if stage == 0:
                to = (y + i) % Y
                out.append(remote(send.at[to, :, c], hop_a.at[y], sems, i, {"gs": gs_of(to, z, c)}))
            elif stage == 1:
                to = (z + i) % Z
                out.append(remote(send.at[:, to, 1 - c], hop_b.at[z], sems, i, {"gs": gs_of(y, to, 1 - c)}))
            elif stage == 2:
                to = (z + i) % Z
                out.append(remote(hop_a.at[:, to], recv.at[:, z, c], sems, i, {"gs": gs_of(y, to, c)}))
            else:
                to = (y + i) % Y
                out.append(remote(hop_b.at[:, to], recv.at[y, :, 1 - c], sems, i, {"gs": gs_of(to, z, c)}))
        return out

    def each(self, stage, act):
        def body(i):
            for copy in self.copies(stage, i):
                act(copy)

        loop(0 if stage == 1 else 1, 8, body)

    def start(self, stage):
        self.each(stage, lambda copy: copy.start())

    def arrive(self, stage):
        self.each(stage, lambda copy: copy.wait_recv())

    def sent(self):
        for stage in range(4):
            self.each(stage, lambda copy: copy.wait_send())

    def keep_first(self):
        y, z, c, _ = place()
        for send, hop_a, hop_b, recv in self.pairs:
            hop_a[y] = send[y, :, c]

    def keep_a(self):
        y, z, c, _ = place()
        for send, hop_a, hop_b, recv in self.pairs:
            recv[:, z, c] = hop_a[:, z]

    def keep_b(self):
        y, z, c, _ = place()
        for send, hop_a, hop_b, recv in self.pairs:
            recv[y, :, 1 - c] = hop_b[:, y]


def step_kernel(
    scale, lists_ref, lengths_ref, order_ref, feat_ref, geo_in_ref, decoder_ref, images_ref,
    teacher_hbm, basis_hbm, moments_hbm, tables_hbm,
    feat_out, geo_out, dec_out,
    teacher_ref, basis_ref, moments_ref, tables_ref, load_sems,
    onehot, select, mask, source, gathered,
    fsend_f, fsend_g, fa_f, fa_g, fb_f, fb_g, frecv_f, frecv_g, forward_sems,
    geo_rows, geo, geo_grad, rows, columns, feat_t, alphas, weights, weights_b, inners, values, bias, totals, carry,
    terms, right, acc, dec,
    rsend_f, rsend_g, ra_f, ra_g, rb_f, rb_g, rrecv_f, rrecv_g, return_sems,
    dec_tiles, d1, p1, d2, p2, d3, p3, d4, d5, sum_sems,
    returned, shares, view_in, view_sems,
):
    y, z, c, x = place()
    count = feat_ref.shape[0]
    tiles = lists_ref.shape[0]
    nblocks = count // BLK
    corner = x * C + c

    loads = [
        pltpu.make_async_copy(src, dst, load_sems.at[n])
        for n, (src, dst) in enumerate((
            (teacher_hbm, teacher_ref), (basis_hbm, basis_ref), (moments_hbm, moments_ref), (tables_hbm, tables_ref)
        ))
    ]
    for load in loads:
        load.start()

    barrier = pltpu.get_barrier_semaphore()

    def greet(start, stop, target):
        loop(start, stop, lambda i: pl.semaphore_signal(
            barrier, inc=1, device_id=target(i), device_id_type=pl.DeviceIdType.MESH))

    greet(1, Y, lambda i: {"gs": gs_of((y + i) % Y, z, c)})
    greet(1, Z, lambda i: {"gs": gs_of(y, (z + i) % Z, c)})
    greet(0, Z, lambda i: {"gs": gs_of(y, (z + i) % Z, 1 - c)})
    greet(1, X, lambda i: {"gs": gs_of(y, z, c), "view": (x + i) % X})
    greet(1, X, lambda i: {"gs": gs_of(y, z, 1 - c), "view": (x + i) % X})

    row = lax.broadcasted_iota(jnp.int32, (128, count), 0)
    column = lax.broadcasted_iota(jnp.int32, (128, count), 1)
    select[...] = jnp.where(row == jnp.right_shift(column, 3), 1.0, 0.0).astype(BF16)
    mask[...] = jnp.where(jnp.right_shift(row, 4) == jnp.bitwise_and(column, 7), 1.0, 0.0)
    for n in range(nblocks):
        span = slice(n * BLK, (n + 1) * BLK)
        source[0:FEAT, span] = feat_ref[span, :].astype(F32).T.astype(BF16)
    padded = jnp.concatenate([geo_in_ref[n] for n in range(9)] + [jnp.zeros((7, count), F32)], 0)
    for index, part in enumerate(pieces(padded, 3)):
        source[FEAT + 16 * index : FEAT + 16 * index + 16, :] = part
    step = 2 * Z * C * SEND
    for n in range(count // step):
        span = slice(n * step, (n + 1) * step)
        row = lax.broadcasted_iota(jnp.int32, (count, step), 0)
        hot = jnp.where(row == order_ref[:, span], 1.0, 0.0).astype(BF16)
        onehot[:, span] = hot
        picked = dot(source[...], hot)
        fsend_f[n * 2 : n * 2 + 2] = picked[0:FEAT, :].T.reshape(2, Z, C, SEND, FEAT).astype(BF16)
        gathered[:, span] = picked[FEAT : FEAT + 48, :]
    sent_rows = to_rows([gathered[16 * i : 16 * i + 16, :] for i in range(3)], select[...], mask[...])
    for d in range(Y * Z * C):
        fsend_g[d // (Z * C), (d // C) % Z, d % C] = sent_rows[d : d + 1, :]

    pl.semaphore_wait(barrier, Y - 1 + Z - 1 + Z + 2 * (X - 1))
    forward = Exchange([(fsend_f, fa_f, fb_f, frecv_f), (fsend_g, fa_g, fb_g, frecv_g)], forward_sems)
    forward.start(0)
    forward.start(1)
    forward.keep_first()
    acc[...] = jnp.zeros_like(acc)
    dec[...] = jnp.zeros_like(dec)
    rows[...] = jnp.zeros_like(rows)
    forward.arrive(0)
    forward.start(2)
    forward.keep_a()
    forward.arrive(1)
    forward.start(3)
    forward.keep_b()
    for load in loads:
        load.wait()
    forward.arrive(2)
    forward.arrive(3)

    for d in range(Y * Z * C):
        geo_rows[d : d + 1, :] = frecv_g[d // (Z * C), (d // C) % Z, d % C]
    geo[...] = from_rows(geo_rows[...], select[...], mask[...])
    shard = lax.axis_index("gs")
    center_x = (2 * TS * (shard % 30) + TS).astype(F32)
    center_y = (2 * TS * (shard // 30) + TS).astype(F32)

    def parameters():
        gx = jnp.clip(geo[0:1, :] - center_x, -4096.0, 4096.0)
        gy = jnp.clip(geo[1:2, :] - center_y, -4096.0, 4096.0)
        ca = jnp.exp(geo[2:3, :])
        cc = jnp.exp(geo[3:4, :])
        slope = jnp.tanh(geo[4:5, :])
        reach = 0.8 * jnp.exp(0.5 * (geo[2:3, :] + geo[3:4, :]))
        return gx, gy, ca, cc, slope, reach

    gx, gy, ca, cc, slope, reach = parameters()
    cb = slope * reach
    linear_x = ca * gx + cb * gy
    linear_y = cb * gx + cc * gy
    constant = -jnp.log(1.0 + jnp.exp(-geo[5:6, :])) - 0.5 * (gx * linear_x + gy * linear_y)
    at = 32
    for coefficient, repeats in (
        (constant, 1), (linear_x, 1), (linear_y, 1), (-0.5 * ca, 2), (-cb, 2), (-0.5 * cc, 2)
    ):
        parts = pieces(coefficient * LOG2E, 3)
        for _ in range(repeats):
            for part in parts:
                rows[at : at + 1, :] = part.astype(F32)
                at += 1
    high, middle, low = pieces(geo[6:9, :], 3)
    for index, part in enumerate((high, high, middle, high, middle, low)):
        rows[3 * index : 3 * index + 3, :] = part.astype(F32)
    for n in range(nblocks):
        span = slice(n * BLK, (n + 1) * BLK)
        block = frecv_f[n].astype(F32).reshape(BLK, FEAT)
        columns[span, 0:FEAT] = block.astype(BF16)
        columns[span, FEAT : 2 * FEAT] = rows[:, span].T.astype(BF16)
        feat_t[0:FEAT, span] = block.T.astype(BF16)
        feat_t[FEAT : FEAT + 32, span] = rows[0:32, span].astype(BF16)

    def xc(i):
        to = (corner + i) % (X * C)
        return to, {"gs": gs_of(y, z, to % C), "view": to // C}

    def sum_copy(stage, i):
        sems = sum_sems.at[stage]
        if stage == 0:
            to, target = xc(i)
            return remote(dec_tiles.at[to], d1.at[corner], sems, i, target)
        if stage == 1:
            to = (z + i) % Z
            return remote(p1.at[to], d2.at[z], sems, i, {"gs": gs_of(y, to, c)})
        if stage == 2:
            to = (y + i) % Y
            return remote(p2, d3.at[y], sems, i, {"gs": gs_of(to, z, c)})
        if stage == 3:
            to = (z + i) % Z
            return remote(p3, d4.at[z], sems, i, {"gs": gs_of(y, to, c)})
        to, target = xc(i)
        return remote(d4, d5.at[corner], sems, i, target)

    def sum_start(stage):
        loop(1, 8, lambda i: sum_copy(stage, i).start())

    def sum_arrive(stage):
        loop(1, 8, lambda i: sum_copy(stage, i).wait_recv())

    def tile_step(tile):
        block_i = lax.broadcasted_iota(jnp.int32, (LIST, LIST), 0)
        slot_i = lax.broadcasted_iota(jnp.int32, (LIST, LIST), 1)
        slot_col = jnp.sum(
            jnp.where(block_i == lists_ref[pl.ds(tile, 1), :], slot_i.astype(F32), 0.0), axis=1, keepdims=True
        )
        slot_row = jnp.sum(jnp.where(block_i == slot_i, slot_col, 0.0), axis=0, keepdims=True)
        earlier = jnp.where(slot_row < slot_col, 1.0, 0.0)
        later = jnp.where(slot_row > slot_col, 1.0, 0.0)
        tile_i = lax.broadcasted_iota(jnp.int32, lengths_ref.shape, 1)
        length = jnp.sum(jnp.where(tile_i == tile, lengths_ref[...].astype(F32), 0.0), axis=1, keepdims=True)
        bias[...] = jnp.broadcast_to(jnp.where(slot_col < length, 0.0, -1e30), (LIST, PIX))

        inners[...] = dot(columns[:, FEAT:], basis_ref[tile])
        for n in range(LIST):
            span = slice(n * BLK, (n + 1) * BLK)
            alpha = jnp.exp2(inners[span, :] + bias[n : n + 1, :])
            log_keep = alpha * (
                -LOG2E + alpha * (-LOG2E / 2 + alpha * (-LOG2E / 3 + alpha * (-LOG2E / 4)))
            )
            high, low = pieces(log_keep, 2)
            inner = dot(tables_ref[0], jnp.concatenate([high, low], 0))
            totals[n : n + 1, :] = inner[BLK - 1 : BLK, :] + log_keep[BLK - 1 : BLK, :]
            alphas[span, :] = alpha
            inners[span, :] = inner
        carry[...] = sum(earlier[:, n : n + 1] * totals[n : n + 1, :] for n in range(LIST))
        for n in range(LIST):
            span = slice(n * BLK, (n + 1) * BLK)
            weight = alphas[span, :] * jnp.exp2(inners[span, :] + carry[n : n + 1, :])
            weight_b, weight_low = pieces(weight, 2)
            weights[span, :] = weight
            weights_b[span, 0:PIX] = weight_b
            weights_b[span, PIX : 2 * PIX] = weight_low
        total = dot(feat_t[...], weights_b[:, 0:PIX])
        total_low = dot(feat_t[FEAT:, :], weights_b[:, PIX : 2 * PIX])

        rendered_t = total[0:FEAT, :].astype(BF16)
        color = (
            total[FEAT : FEAT + 3] + total[FEAT + 6 : FEAT + 9] + total[FEAT + 15 : FEAT + 18]
            + total_low[0:3] + total_low[6:9]
        )
        pixels = pl.ds(pl.multiple_of(tile * PIX, PIX), PIX)
        error_color = color - jnp.concatenate([images_ref[n, :, pixels] for n in range(3)], 0)
        gcolor = error_color * lax.rsqrt(error_color * error_color + 0.04)
        pred = dot(total[0:FEAT, :].T.astype(BF16), decoder_ref[...])
        error = pred - teacher_ref[pixels, :].astype(F32)
        gpred = (error * lax.rsqrt(error * error + 0.04)).astype(BF16)
        dec[...] += dot(rendered_t, gpred)

        @pl.when(tile == tiles - 1)
        def _():
            for n in range(FEAT * CT // 1024):
                row, lane = n // (CT // 128), n % (CT // 128)
                dec_tiles[n // Z, n % Z] = dec[8 * row : 8 * row + 8, 128 * lane : 128 * lane + 128]
            sum_start(0)

        terms[0:FEAT, :] = dot_t(decoder_ref[...], gpred)
        terms[FEAT:, :] = jnp.zeros_like(terms[FEAT:, :])
        for index, part in enumerate([pieces(gcolor, 3)[n] for n in (0, 1, 0, 2, 1, 0)]):
            terms[FEAT + 3 * index : FEAT + 3 * index + 3, :] = part.astype(F32)
        right[...] = terms[...].T.astype(BF16)

        values[...] = dot(columns[...], terms[...].astype(BF16))
        for n in range(LIST):
            span = slice(n * BLK, (n + 1) * BLK)
            value = values[span, :] * weights[span, :]
            high, low = pieces(value, 2)
            inner = dot(tables_ref[1], jnp.concatenate([high, low], 0))
            totals[n : n + 1, :] = inner[0:1, :] + value[0:1, :]
            values[span, :] = value
            inners[span, :] = inner
        carry[...] = sum(later[:, n : n + 1] * totals[n : n + 1, :] for n in range(LIST))
        for n in range(LIST):
            span = slice(n * BLK, (n + 1) * BLK)
            alpha = alphas[span, :]
            square = alpha * alpha
            ratio = alpha + square
            ratio = ratio + ratio * square
            ratio = ratio + ratio * (square * square)
            gexponent = values[span, :] - ratio * (inners[span, :] + carry[n : n + 1, :])
            high, low = pieces(gexponent, 2)
            weights_b[span, 2 * PIX : 3 * PIX] = high
            weights_b[span, 3 * PIX : 4 * PIX] = low
        moments = moments_ref[tile]
        acc[...] += dot(weights_b[:, 0:PIX], right[...])
        acc[:, FEAT:] += dot(weights_b[:, PIX:], jnp.concatenate([right[:, FEAT:], moments, moments], 0))

    loop(0, tiles, tile_step)

    backward = Exchange([(rsend_f, ra_f, rb_f, rrecv_f), (rsend_g, ra_g, rb_g, rrecv_g)], return_sems)
    d1[corner] = dec_tiles[corner]
    sum_arrive(0)
    p1[...] = sum(d1[i] for i in range(X * C))
    sum_start(1)
    d2[z] = p1[z]

    for n in range(nblocks):
        span = slice(n * BLK, (n + 1) * BLK)
        rsend_f[n] = acc[span, 0:FEAT].reshape(Z, C, SEND, FEAT)
        rows[:, span] = acc[span, FEAT:].T
    gx, gy, ca, cc, slope, reach = parameters()
    cb = slope * reach
    s0, sx, sy = (rows[32 + i : 33 + i, :] for i in range(3))
    sxx, sxy, syy = (rows[35 + 2 * i : 36 + 2 * i, :] + rows[36 + 2 * i : 37 + 2 * i, :] for i in range(3))
    ux = sx - gx * s0
    uy = sy - gy * s0
    dxx = sxx - 2.0 * gx * sx + gx * gx * s0
    dyy = syy - 2.0 * gy * sy + gy * gy * s0
    dxy = sxy - gx * sy - gy * sx + gx * gy * s0
    geo_grad[0:1, :] = ca * ux + cb * uy
    geo_grad[1:2, :] = cb * ux + cc * uy
    geo_grad[2:3, :] = -0.5 * (ca * dxx + cb * dxy)
    geo_grad[3:4, :] = -0.5 * (cc * dyy + cb * dxy)
    geo_grad[4:5, :] = -dxy * reach * (1.0 - slope * slope)
    geo_grad[5:6, :] = s0 / (1.0 + jnp.exp(geo[5:6, :]))
    geo_grad[6:9, :] = rows[0:3, :] + rows[3:6, :] + rows[9:12, :]
    geo_grad[9:16, :] = jnp.zeros((7, count), F32)
    back_rows = to_rows(pieces(geo_grad[...], 3), select[...], mask[...])
    for d in range(Y * Z * C):
        rsend_g[d // (Z * C), (d // C) % Z, d % C] = back_rows[d : d + 1, :]

    backward.start(0)
    backward.start(1)
    backward.keep_first()
    sum_arrive(1)
    p2[...] = sum(d2[i] for i in range(Z))
    sum_start(2)
    d3[y] = p2[...]
    backward.arrive(0)
    backward.start(2)
    backward.keep_a()
    backward.arrive(1)
    backward.start(3)
    backward.keep_b()
    sum_arrive(2)
    p3[...] = sum(d3[i] for i in range(Y)) * scale
    sum_start(3)
    d4[z] = p3[...]
    sum_arrive(3)
    sum_start(4)
    d5[corner] = d4[...]
    backward.arrive(2)
    backward.arrive(3)

    for d in range(Y * Z * C):
        geo_rows[d : d + 1, :] = rrecv_g[d // (Z * C), (d // C) % Z, d % C]
    geo_back = from_rows(geo_rows[...], select[...], mask[...])
    geo_parts = jnp.concatenate([part.astype(F32) for part in pieces(geo_back, 3)], 0).astype(BF16)
    for n in range(Y):
        high, low = pieces(rrecv_f[n].reshape(Z * C * SEND, FEAT), 2)
        span = slice(n * Z * C * SEND, (n + 1) * Z * C * SEND)
        returned[span, 0:FEAT] = high
        returned[span, FEAT : 2 * FEAT] = low
    quarter = count // X

    def view_copy(i):
        return remote(shares.at[i], view_in.at[x], view_sems, i, {"gs": gs_of(y, z, c), "view": (x + i) % X})

    for i in (2, 1, 3, 0):
        start = pl.multiple_of(((x + i) % X) * quarter, quarter)
        both = dot(onehot[pl.ds(start, quarter), :], returned[...])
        share = both[:, 0:FEAT] + both[:, FEAT : 2 * FEAT]
        if i:
            shares[i] = share
            view_copy(i).start()
        else:
            view_in[x] = share
    own = dot_t(geo_parts, onehot[...])
    own = own[0:16] + own[16:32] + own[32:48]
    for n in range(9):
        geo_out[n] = own[n : n + 1]
    sum_arrive(4)
    for n in range(FEAT * CT // 1024):
        row, lane = n // (CT // 128), n % (CT // 128)
        dec_out[8 * row : 8 * row + 8, 128 * lane : 128 * lane + 128] = d5[n // Z, n % Z]
    for i in (1, 2, 3):
        view_copy(i).wait_recv()
    feat_out[...] = view_in[0] + view_in[1] + view_in[2] + view_in[3]
    for i in (1, 2, 3):
        view_copy(i).wait_send()
    for stage in range(5):
        loop(1, 8, lambda i: sum_copy(stage, i).wait_send())
    forward.sent()
    backward.sent()


def exchange_buffers(dtype):
    geo_dtype = F32
    return [
        pltpu.VMEM((*GROUP, SEND, FEAT), dtype), pltpu.VMEM((*GROUP, 1, 128), geo_dtype),
        pltpu.VMEM((Y, Z, SEND, FEAT), dtype), pltpu.VMEM((Y, Z, 1, 128), geo_dtype),
        pltpu.VMEM((Z, Y, SEND, FEAT), dtype), pltpu.VMEM((Z, Y, 1, 128), geo_dtype),
        pltpu.VMEM((*GROUP, SEND, FEAT), dtype), pltpu.VMEM((*GROUP, 1, 128), geo_dtype),
        pltpu.SemaphoreType.DMA((8, 2, 8)),
    ]


def on_device(features, geometry, decoder, teacher, images, send_index, tile_lists, tile_lengths):
    count = features.shape[0]
    tiles = tile_lists.shape[1]
    quarter = count // X
    basis, moments = pixel_tables(tiles)
    tables = order_tables()
    scale = 1.0 / math.sqrt(lax.axis_size("gs") * lax.axis_size("view") * tiles * PIX)
    vmem = pl.BlockSpec(memory_space=pltpu.VMEM)
    hbm = pl.BlockSpec(memory_space=pl.ANY)
    tile = (8, 128)
    feature_grad, geo_own, decoder_grad = pl.pallas_call(
        functools.partial(step_kernel, scale),
        in_specs=[vmem] * 7 + [hbm] * 4,
        out_specs=[vmem] * 3,
        out_shape=[
            jax.ShapeDtypeStruct((quarter, FEAT), F32),
            jax.ShapeDtypeStruct((9, 1, count), F32),
            jax.ShapeDtypeStruct((FEAT, CT), F32),
        ],
        scratch_shapes=[
            pltpu.VMEM((tiles * PIX, CT), BF16),
            pltpu.VMEM(basis.shape, BF16),
            pltpu.VMEM(moments.shape, BF16),
            pltpu.VMEM(tables.shape, BF16),
            pltpu.SemaphoreType.DMA((4,)),
            pltpu.VMEM((count, count), BF16),
            pltpu.VMEM((128, count), BF16),
            pltpu.VMEM((128, count), F32),
            pltpu.VMEM((FEAT + 48, count), BF16),
            pltpu.VMEM((48, count), F32),
            *exchange_buffers(BF16),
            pltpu.VMEM((128, 128), F32),
            pltpu.VMEM((16, count), F32),
            pltpu.VMEM((16, count), F32),
            pltpu.VMEM((128, count), F32),
            pltpu.VMEM((count, 2 * FEAT), BF16),
            pltpu.VMEM((FEAT + 32, count), BF16),
            pltpu.VMEM((LIST * BLK, PIX), F32),
            pltpu.VMEM((LIST * BLK, PIX), F32),
            pltpu.VMEM((LIST * BLK, 4 * PIX), BF16),
            pltpu.VMEM((LIST * BLK, PIX), F32),
            pltpu.VMEM((LIST * BLK, PIX), F32),
            pltpu.VMEM((LIST, PIX), F32),
            pltpu.VMEM((LIST, PIX), F32),
            pltpu.VMEM((LIST, PIX), F32),
            pltpu.VMEM((2 * FEAT, PIX), F32),
            pltpu.VMEM((PIX, 2 * FEAT), BF16),
            pltpu.VMEM((count, 2 * FEAT), F32),
            pltpu.VMEM((FEAT, CT), F32),
            *exchange_buffers(F32),
            pltpu.VMEM((X * C, Z, *tile), F32),
            pltpu.VMEM((X * C, Z, *tile), F32),
            pltpu.VMEM((Z, *tile), F32),
            pltpu.VMEM((Z, *tile), F32),
            pltpu.VMEM(tile, F32),
            pltpu.VMEM((Y, *tile), F32),
            pltpu.VMEM(tile, F32),
            pltpu.VMEM((Z, *tile), F32),
            pltpu.VMEM((X * C, Z, *tile), F32),
            pltpu.SemaphoreType.DMA((5, 2, 8)),
            pltpu.VMEM((count, 2 * FEAT), BF16),
            pltpu.VMEM((X, quarter, FEAT), F32),
            pltpu.VMEM((X, quarter, FEAT), F32),
            pltpu.SemaphoreType.DMA((2, X)),
        ],
        compiler_params=pltpu.CompilerParams(
            collective_id=0, has_side_effects=True, vmem_limit_bytes=48 * 1024 * 1024
        ),
        name="step",
    )(
        tile_lists[0], tile_lengths, send_index[0], features, geometry.reshape(9, 1, count), decoder,
        images.reshape(3, 1, tiles * PIX), teacher[0],
        jnp.asarray(basis), jnp.asarray(moments), jnp.asarray(tables),
    )
    return (feature_grad, geo_own.reshape(1, 9, count), decoder_grad)


def solution(mesh):
    placed = (
        P("gs", None),
        P("view", None, "gs"),
        P(),
        P("view", "gs", None),
        P("view", None, "gs"),
        P("view", "gs", None),
        P("view", "gs", None),
        P("view", "gs"),
    )
    return jax.shard_map(
        on_device,
        mesh=mesh,
        in_specs=placed,
        out_specs=(P(("gs", "view"), None), P("view", None, "gs"), P()),
        check_vma=False,
    )
```

```python
import functools
import math

import jax
import jax.numpy as jnp
import numpy as np
from jax import lax
from jax.experimental import pallas as pl
from jax.experimental.pallas import tpu as pltpu
from jax.sharding import PartitionSpec as P

FEAT = 128
CT = 512
TS = 16
BLK = 128
LIST = 8
PIX = TS * TS
SEND = 8
Y, Z, C, X = 8, 8, 2, 4
GROUP = (Y, Z, C)
F32 = jnp.float32
BF16 = jnp.bfloat16
LOG2E = 1.4426950408889634


def pixel_tables(tiles):
    q = np.arange(PIX)
    basis = np.zeros((tiles, 128, PIX), np.float32)
    moments = np.zeros((tiles, PIX, 128), np.float32)
    for k in range(tiles):
        px = TS * (k % 2) + q % TS + 0.5 - TS
        py = TS * (k // 2) + q // TS + 0.5 - TS
        rows = [np.ones(PIX), px, py]
        for square in (px * px, px * py, py * py):
            high = square.astype(jnp.bfloat16).astype(np.float64)
            rows += [high, square - high]
        row = 32
        for index, values in enumerate(rows):
            basis[k, row : row + 3] = values
            row += 3
            moments[k, :, 32 + index] = values
    return basis.astype(jnp.bfloat16), moments.astype(jnp.bfloat16)


def order_tables():
    i = np.arange(BLK)
    before = (i[None, :] < i[:, None]).astype(np.float32)
    after = (i[None, :] > i[:, None]).astype(np.float32)
    return np.stack(
        [np.concatenate([before, before], 1), np.concatenate([after, after], 1)]
    ).astype(jnp.bfloat16)


def pieces(x, count):
    parts = []
    for _ in range(count):
        part = x.astype(BF16)
        parts.append(part)
        x = x - part.astype(F32)
    return parts


def dot(a, b):
    return jnp.dot(a, b, preferred_element_type=F32)


def dot_t(a, b):
    return lax.dot_general(a, b, (((1,), (1,)), ((), ())), preferred_element_type=F32)


def to_rows(parts, select, mask):
    total = None
    for part in parts:
        tiled = (jnp.concatenate([part.astype(F32)] * SEND, 0) * mask).astype(BF16)
        term = dot_t(select, tiled)
        total = term if total is None else total + term
    return total


def from_rows(x, select, mask):
    total = sum(dot(part, select) for part in pieces(x.T, 3)) * mask
    return sum(total[16 * p : 16 * p + 16, :] for p in range(SEND))


def place():
    index = lax.axis_index("gs")
    return index // (Z * C), (index // C) % Z, index % C, lax.axis_index("view")


def gs_of(y, z, c):
    return (y * Z + z) * C + c


def loop(start, stop, body):
    def step(i, carry):
        body(i)
        return carry

    lax.fori_loop(start, stop, step, 0)


def remote(src, dst, sems, i, target):
    return pltpu.make_async_remote_copy(
        src_ref=src, dst_ref=dst, send_sem=sems.at[0, i], recv_sem=sems.at[1, i],
        device_id=target, device_id_type=pl.DeviceIdType.MESH,
    )


class Exchange:
    def __init__(self, send, hop_a, hop_b, recv, sems):
        self.send, self.hop_a, self.hop_b, self.recv, self.sems = send, hop_a, hop_b, recv, sems

    def copy(self, stage, i):
        y, z, c, _ = place()
        sems = self.sems.at[stage]
        if stage == 0:
            to = (y + i) % Y
            return remote(self.send.at[to, :, c], self.hop_a.at[y], sems, i, {"gs": gs_of(to, z, c)})
        if stage == 1:
            to = (z + i) % Z
            return remote(self.send.at[:, to, 1 - c], self.hop_b.at[z], sems, i, {"gs": gs_of(y, to, 1 - c)})
        if stage == 2:
            to = (z + i) % Z
            return remote(self.hop_a.at[:, to], self.recv.at[:, z, c], sems, i, {"gs": gs_of(y, to, c)})
        to = (y + i) % Y
        return remote(self.hop_b.at[:, to], self.recv.at[y, :, 1 - c], sems, i, {"gs": gs_of(to, z, c)})

    def each(self, stage, act):
        loop(0 if stage == 1 else 1, 8, lambda i: act(self.copy(stage, i)))

    def start(self, stage):
        self.each(stage, lambda copy: copy.start())

    def arrive(self, stage):
        self.each(stage, lambda copy: copy.wait_recv())

    def sent(self):
        for stage in range(4):
            self.each(stage, lambda copy: copy.wait_send())

    def keep_first(self):
        y, z, c, _ = place()
        self.hop_a[y] = self.send[y, :, c]

    def keep_a(self):
        y, z, c, _ = place()
        self.recv[:, z, c] = self.hop_a[:, z]

    def keep_b(self):
        y, z, c, _ = place()
        self.recv[y, :, 1 - c] = self.hop_b[:, y]


def step_kernel(
    scale, *refs,
):
    inputs, (feat_out, geo_out, dec_out), held, rest = refs[:11], refs[11:14], refs[14:25], refs[25:]
    (
        order_ref, feat_ref, geo_in_ref, decoder_ref, images_ref, lists_ref, lengths_ref,
        teacher_ref, basis_ref, moments_ref, tables_ref,
    ) = held
    (
        load_sems,
        onehot, select, mask, source, gathered,
        fsend_f, fsend_g, fa_f, fa_g, fb_f, fb_g, frecv_f, frecv_g, forward_sems_f, forward_sems_g,
        geo_rows, geo, geo_grad, rows, columns, feat_t, alphas, weights, weights_b, gparts, inners, values, bias, totals, carry,
        laters, terms, left, right, acc, dec,
        rsend_f, rsend_g, ra_f, ra_g, rb_f, rb_g, rrecv_f, rrecv_g, return_sems_f, return_sems_g,
        dec_tiles, d1, p1, d2, p2, d3, p3, d4, d5, sum_sems,
        returned, shares, view_in, view_sems,
    ) = rest
    y, z, c, x = place()
    count = feat_ref.shape[0]
    tiles = lists_ref.shape[0]
    nblocks = count // BLK
    corner = x * C + c

    loads = [
        pltpu.make_async_copy(src, dst, load_sems.at[n]) for n, (src, dst) in enumerate(zip(inputs, held))
    ]
    for load in loads:
        load.start()

    barrier = pltpu.get_barrier_semaphore()

    def greet(start, stop, target):
        loop(start, stop, lambda i: pl.semaphore_signal(
            barrier, inc=1, device_id=target(i), device_id_type=pl.DeviceIdType.MESH))

    greet(1, Y, lambda i: {"gs": gs_of((y + i) % Y, z, c)})
    greet(1, Z, lambda i: {"gs": gs_of(y, (z + i) % Z, c)})
    greet(0, Z, lambda i: {"gs": gs_of(y, (z + i) % Z, 1 - c)})
    greet(1, X, lambda i: {"gs": gs_of(y, z, c), "view": (x + i) % X})
    greet(1, X, lambda i: {"gs": gs_of(y, z, 1 - c), "view": (x + i) % X})

    for load in loads[:3]:
        load.wait()
    row = lax.broadcasted_iota(jnp.int32, (128, count), 0)
    column = lax.broadcasted_iota(jnp.int32, (128, count), 1)
    select[...] = jnp.where(row == jnp.right_shift(column, 3), 1.0, 0.0).astype(BF16)
    mask[...] = jnp.where(jnp.right_shift(row, 4) == jnp.bitwise_and(column, 7), 1.0, 0.0)
    padded = jnp.concatenate([geo_in_ref[n] for n in range(9)] + [jnp.zeros((7, count), F32)], 0)
    source[...] = jnp.concatenate([part.astype(F32) for part in pieces(padded, 3)], 0).astype(BF16)
    step = 2 * Z * C * SEND
    for n in range(count // step):
        span = slice(n * step, (n + 1) * step)
        row = lax.broadcasted_iota(jnp.int32, (count, step), 0)
        hot = jnp.where(row == order_ref[:, span], 1.0, 0.0).astype(BF16)
        onehot[:, span] = hot
        gathered[:, span] = dot(source[...], hot)
    sent_rows = to_rows([gathered[16 * i : 16 * i + 16, :] for i in range(3)], select[...], mask[...])
    for d in range(Y * Z * C):
        fsend_g[d // (Z * C), (d // C) % Z, d % C] = sent_rows[d : d + 1, :]

    pl.semaphore_wait(barrier, Y - 1 + Z - 1 + Z + 2 * (X - 1))
    forward_g = Exchange(fsend_g, fa_g, fb_g, frecv_g, forward_sems_g)
    forward_f = Exchange(fsend_f, fa_f, fb_f, frecv_f, forward_sems_f)
    forward_g.start(0)
    forward_g.start(1)
    forward_g.keep_first()
    turned = feat_ref[...].astype(F32).T.astype(BF16)
    for n in range(count // step):
        picked = dot(turned, onehot[:, n * step : (n + 1) * step])
        fsend_f[n * 2 : n * 2 + 2] = picked.T.reshape(2, Z, C, SEND, FEAT).astype(BF16)
    forward_f.start(0)
    forward_f.start(1)
    forward_f.keep_first()
    forward_g.arrive(0)
    forward_g.start(2)
    forward_g.keep_a()
    forward_g.arrive(1)
    forward_g.start(3)
    forward_g.keep_b()
    acc[...] = jnp.zeros_like(acc)
    dec[...] = jnp.zeros_like(dec)
    rows[...] = jnp.zeros_like(rows)
    forward_f.arrive(0)
    forward_f.start(2)
    forward_f.keep_a()
    forward_f.arrive(1)
    forward_f.start(3)
    forward_f.keep_b()
    for load in loads[3:]:
        load.wait()
    forward_g.arrive(2)
    forward_g.arrive(3)

    for d in range(Y * Z * C):
        geo_rows[d : d + 1, :] = frecv_g[d // (Z * C), (d // C) % Z, d % C]
    geo[...] = from_rows(geo_rows[...], select[...], mask[...])
    shard = lax.axis_index("gs")
    center_x = (2 * TS * (shard % 30) + TS).astype(F32)
    center_y = (2 * TS * (shard // 30) + TS).astype(F32)

    def parameters():
        gx = jnp.clip(geo[0:1, :] - center_x, -4096.0, 4096.0)
        gy = jnp.clip(geo[1:2, :] - center_y, -4096.0, 4096.0)
        ca = jnp.exp(geo[2:3, :])
        cc = jnp.exp(geo[3:4, :])
        slope = jnp.tanh(geo[4:5, :])
        reach = 0.8 * jnp.exp(0.5 * (geo[2:3, :] + geo[3:4, :]))
        return gx, gy, ca, cc, slope, reach

    gx, gy, ca, cc, slope, reach = parameters()
    cb = slope * reach
    linear_x = ca * gx + cb * gy
    linear_y = cb * gx + cc * gy
    constant = -jnp.log(1.0 + jnp.exp(-geo[5:6, :])) - 0.5 * (gx * linear_x + gy * linear_y)
    at = 32
    for coefficient, repeats in (
        (constant, 1), (linear_x, 1), (linear_y, 1), (-0.5 * ca, 2), (-cb, 2), (-0.5 * cc, 2)
    ):
        parts = pieces(coefficient * LOG2E, 3)
        for _ in range(repeats):
            for part in parts:
                rows[at : at + 1, :] = part.astype(F32)
                at += 1
    high, middle, low = pieces(geo[6:9, :], 3)
    for index, part in enumerate((high, high, middle, high, middle, low)):
        rows[3 * index : 3 * index + 3, :] = part.astype(F32)
    for n in range(nblocks):
        span = slice(n * BLK, (n + 1) * BLK)
        columns[span, FEAT : 2 * FEAT] = rows[:, span].T.astype(BF16)
    feat_t[FEAT : FEAT + 32, :] = rows[0:32, :].astype(BF16)

    def xc(i):
        to = (corner + i) % (X * C)
        return to, {"gs": gs_of(y, z, to % C), "view": to // C}

    def sum_copy(stage, i):
        sems = sum_sems.at[stage]
        if stage == 0:
            to, target = xc(i)
            return remote(dec_tiles.at[to], d1.at[corner], sems, i, target)
        if stage == 1:
            to = (z + i) % Z
            return remote(p1.at[to], d2.at[z], sems, i, {"gs": gs_of(y, to, c)})
        if stage == 2:
            to = (y + i) % Y
            return remote(p2, d3.at[y], sems, i, {"gs": gs_of(to, z, c)})
        if stage == 3:
            to = (z + i) % Z
            return remote(p3, d4.at[z], sems, i, {"gs": gs_of(y, to, c)})
        to, target = xc(i)
        return remote(d4, d5.at[corner], sems, i, target)

    def sum_start(stage):
        loop(1, 8, lambda i: sum_copy(stage, i).start())

    def sum_arrive(stage):
        loop(1, 8, lambda i: sum_copy(stage, i).wait_recv())

    def sum_step(stage):
        sum_arrive(stage)
        if stage == 0:
            p1[...] = sum(d1[i] for i in range(X * C))
            sum_start(1)
            d2[z] = p1[z]
        elif stage == 1:
            p2[...] = sum(d2[i] for i in range(Z))
            sum_start(2)
            d3[y] = p2[...]
        elif stage == 2:
            p3[...] = sum(d3[i] for i in range(Y)) * scale
            sum_start(3)
            d4[z] = p3[...]
        else:
            sum_start(4)
            d5[corner] = d4[...]

    def weigh(tile):
        block_i = lax.broadcasted_iota(jnp.int32, (LIST, LIST), 0)
        slot_i = lax.broadcasted_iota(jnp.int32, (LIST, LIST), 1)
        slot_col = jnp.sum(
            jnp.where(block_i == lists_ref[pl.ds(tile, 1), :], slot_i.astype(F32), 0.0), axis=1, keepdims=True
        )
        slot_row = jnp.sum(jnp.where(block_i == slot_i, slot_col, 0.0), axis=0, keepdims=True)
        earlier = jnp.where(slot_row < slot_col, 1.0, 0.0)
        laters[tile] = jnp.where(slot_row > slot_col, 1.0, 0.0)
        tile_i = lax.broadcasted_iota(jnp.int32, lengths_ref.shape, 1)
        length = jnp.sum(jnp.where(tile_i == tile, lengths_ref[...].astype(F32), 0.0), axis=1, keepdims=True)
        bias[...] = jnp.broadcast_to(jnp.where(slot_col < length, 0.0, -1e30), (LIST, PIX))

        inners[...] = dot(columns[:, FEAT:], basis_ref[tile])
        for n in range(LIST):
            span = slice(n * BLK, (n + 1) * BLK)
            alpha = jnp.exp2(inners[span, :] + bias[n : n + 1, :])
            log_keep = alpha * (
                -LOG2E + alpha * (-LOG2E / 2 + alpha * (-LOG2E / 3 + alpha * (-LOG2E / 4)))
            )
            high, low = pieces(log_keep, 2)
            inner = dot(tables_ref[0], jnp.concatenate([high, low], 0))
            totals[n : n + 1, :] = inner[BLK - 1 : BLK, :] + log_keep[BLK - 1 : BLK, :]
            alphas[tile, span, :] = alpha
            inners[span, :] = inner
        carry[...] = sum(earlier[:, n : n + 1] * totals[n : n + 1, :] for n in range(LIST))
        for n in range(LIST):
            span = slice(n * BLK, (n + 1) * BLK)
            weight = alphas[tile, span, :] * jnp.exp2(inners[span, :] + carry[n : n + 1, :])
            weight_b, weight_low = pieces(weight, 2)
            weights[tile, span, :] = weight
            weights_b[tile, span, 0:PIX] = weight_b
            weights_b[tile, span, PIX : 2 * PIX] = weight_low
    def render(tile):
        total = dot(feat_t[...], weights_b[tile, :, 0:PIX])
        total_low = dot(feat_t[FEAT:, :], weights_b[tile, :, PIX : 2 * PIX])

        rendered_t = total[0:FEAT, :].astype(BF16)
        color = (
            total[FEAT : FEAT + 3] + total[FEAT + 6 : FEAT + 9] + total[FEAT + 15 : FEAT + 18]
            + total_low[0:3] + total_low[6:9]
        )
        pixels = pl.ds(pl.multiple_of(tile * PIX, PIX), PIX)
        error_color = color - jnp.concatenate([images_ref[n, :, pixels] for n in range(3)], 0)
        gcolor = error_color * lax.rsqrt(error_color * error_color + 0.04)
        pred = dot(total[0:FEAT, :].T.astype(BF16), decoder_ref[...])
        error = pred - teacher_ref[pixels, :].astype(F32)
        gpred = (error * lax.rsqrt(error * error + 0.04)).astype(BF16)
        dec[...] += dot(rendered_t, gpred)

        terms[0:FEAT, :] = dot_t(decoder_ref[...], gpred)
        terms[FEAT:, :] = jnp.zeros_like(terms[FEAT:, :])
        for index, part in enumerate([pieces(gcolor, 3)[n] for n in (0, 1, 0, 2, 1, 0)]):
            terms[FEAT + 3 * index : FEAT + 3 * index + 3, :] = part.astype(F32)
        left[tile] = terms[...].astype(BF16)
        right[tile] = terms[...].T.astype(BF16)

    def differentiate(tile):
        values[...] = dot(columns[...], left[tile])
        for n in range(LIST):
            span = slice(n * BLK, (n + 1) * BLK)
            value = values[span, :] * weights[tile, span, :]
            high, low = pieces(value, 2)
            inner = dot(tables_ref[1], jnp.concatenate([high, low], 0))
            totals[n : n + 1, :] = inner[0:1, :] + value[0:1, :]
            values[span, :] = value
            inners[span, :] = inner
        later = laters[tile]
        carry[...] = sum(later[:, n : n + 1] * totals[n : n + 1, :] for n in range(LIST))
        for n in range(LIST):
            span = slice(n * BLK, (n + 1) * BLK)
            alpha = alphas[tile, span, :]
            square = alpha * alpha
            ratio = alpha + square
            ratio = ratio + ratio * square
            ratio = ratio + ratio * (square * square)
            gexponent = values[span, :] - ratio * (inners[span, :] + carry[n : n + 1, :])
            high, low = pieces(gexponent, 2)
            gparts[span, 0:PIX] = high
            gparts[span, PIX : 2 * PIX] = low
        moments = moments_ref[tile]
        acc[...] += dot(weights_b[tile, :, 0:PIX], right[tile])
        acc[:, FEAT:] += dot(weights_b[tile, :, PIX:], right[tile, :, FEAT:]) + dot(
            gparts[...], jnp.concatenate([moments, moments], 0)
        )
        for stage in range(3):

            @pl.when(tile == stage + 1)
            def _():
                sum_step(stage)

    loop(0, tiles, weigh)
    forward_f.arrive(2)
    forward_f.arrive(3)
    for n in range(nblocks):
        span = slice(n * BLK, (n + 1) * BLK)
        block = frecv_f[n].astype(F32).reshape(BLK, FEAT)
        columns[span, 0:FEAT] = block.astype(BF16)
        feat_t[0:FEAT, span] = block.T.astype(BF16)
    loop(0, tiles, render)
    for n in range(FEAT * CT // 1024):
        row, lane = n // (CT // 128), n % (CT // 128)
        dec_tiles[n // Z, n % Z] = dec[8 * row : 8 * row + 8, 128 * lane : 128 * lane + 128]
    sum_start(0)
    d1[corner] = dec_tiles[corner]
    loop(0, tiles, differentiate)

    backward_f = Exchange(rsend_f, ra_f, rb_f, rrecv_f, return_sems_f)
    backward_g = Exchange(rsend_g, ra_g, rb_g, rrecv_g, return_sems_g)
    for n in range(nblocks):
        rsend_f[n] = acc[n * BLK : (n + 1) * BLK, 0:FEAT].reshape(Z, C, SEND, FEAT)
    backward_f.start(0)
    backward_f.start(1)
    backward_f.keep_first()
    for n in range(nblocks):
        span = slice(n * BLK, (n + 1) * BLK)
        rows[:, span] = acc[span, FEAT:].T
    gx, gy, ca, cc, slope, reach = parameters()
    cb = slope * reach
    s0, sx, sy = (rows[32 + i : 33 + i, :] for i in range(3))
    sxx, sxy, syy = (rows[35 + 2 * i : 36 + 2 * i, :] + rows[36 + 2 * i : 37 + 2 * i, :] for i in range(3))
    ux = sx - gx * s0
    uy = sy - gy * s0
    dxx = sxx - 2.0 * gx * sx + gx * gx * s0
    dyy = syy - 2.0 * gy * sy + gy * gy * s0
    dxy = sxy - gx * sy - gy * sx + gx * gy * s0
    geo_grad[0:1, :] = ca * ux + cb * uy
    geo_grad[1:2, :] = cb * ux + cc * uy
    geo_grad[2:3, :] = -0.5 * (ca * dxx + cb * dxy)
    geo_grad[3:4, :] = -0.5 * (cc * dyy + cb * dxy)
    geo_grad[4:5, :] = -dxy * reach * (1.0 - slope * slope)
    geo_grad[5:6, :] = s0 / (1.0 + jnp.exp(geo[5:6, :]))
    geo_grad[6:9, :] = rows[0:3, :] + rows[3:6, :] + rows[9:12, :]
    geo_grad[9:16, :] = jnp.zeros((7, count), F32)
    back_rows = to_rows(pieces(geo_grad[...], 3), select[...], mask[...])
    for d in range(Y * Z * C):
        rsend_g[d // (Z * C), (d // C) % Z, d % C] = back_rows[d : d + 1, :]

    backward_g.start(0)
    backward_g.start(1)
    backward_g.keep_first()
    sum_step(3)
    backward_f.arrive(0)
    backward_f.start(2)
    backward_f.keep_a()
    backward_f.arrive(1)
    backward_f.start(3)
    backward_f.keep_b()
    backward_g.arrive(0)
    backward_g.start(2)
    backward_g.keep_a()
    backward_g.arrive(1)
    backward_g.start(3)
    backward_g.keep_b()
    sum_arrive(4)
    for n in range(FEAT * CT // 1024):
        row, lane = n // (CT // 128), n % (CT // 128)
        dec_out[8 * row : 8 * row + 8, 128 * lane : 128 * lane + 128] = d5[n // Z, n % Z]
    backward_f.arrive(2)
    backward_f.arrive(3)

    for n in range(Y):
        high, low = pieces(rrecv_f[n].reshape(Z * C * SEND, FEAT), 2)
        span = slice(n * Z * C * SEND, (n + 1) * Z * C * SEND)
        returned[span, 0:FEAT] = high
        returned[span, FEAT : 2 * FEAT] = low
    quarter = count // X

    def view_copy(i):
        return remote(shares.at[i], view_in.at[x], view_sems, i, {"gs": gs_of(y, z, c), "view": (x + i) % X})

    for i in (2, 1, 3, 0):
        start = pl.multiple_of(((x + i) % X) * quarter, quarter)
        both = dot(onehot[pl.ds(start, quarter), :], returned[...])
        share = both[:, 0:FEAT] + both[:, FEAT : 2 * FEAT]
        if i:
            shares[i] = share
            view_copy(i).start()
        else:
            view_in[x] = share
    backward_g.arrive(2)
    backward_g.arrive(3)
    for d in range(Y * Z * C):
        geo_rows[d : d + 1, :] = rrecv_g[d // (Z * C), (d // C) % Z, d % C]
    geo_back = from_rows(geo_rows[...], select[...], mask[...])
    geo_parts = jnp.concatenate([part.astype(F32) for part in pieces(geo_back, 3)], 0).astype(BF16)
    own = dot_t(geo_parts, onehot[...])
    own = own[0:16] + own[16:32] + own[32:48]
    for n in range(9):
        geo_out[n] = own[n : n + 1]
    for i in (1, 2, 3):
        view_copy(i).wait_recv()
    feat_out[...] = view_in[0] + view_in[1] + view_in[2] + view_in[3]
    for i in (1, 2, 3):
        view_copy(i).wait_send()
    for stage in range(5):
        loop(1, 8, lambda i: sum_copy(stage, i).wait_send())
    for exchange in (forward_f, forward_g, backward_f, backward_g):
        exchange.sent()


def exchange_buffers(dtype):
    geo_dtype = F32
    return [
        pltpu.VMEM((*GROUP, SEND, FEAT), dtype), pltpu.VMEM((*GROUP, 1, 128), geo_dtype),
        pltpu.VMEM((Y, Z, SEND, FEAT), dtype), pltpu.VMEM((Y, Z, 1, 128), geo_dtype),
        pltpu.VMEM((Z, Y, SEND, FEAT), dtype), pltpu.VMEM((Z, Y, 1, 128), geo_dtype),
        pltpu.VMEM((*GROUP, SEND, FEAT), dtype), pltpu.VMEM((*GROUP, 1, 128), geo_dtype),
        pltpu.SemaphoreType.DMA((4, 2, 8)), pltpu.SemaphoreType.DMA((4, 2, 8)),
    ]


def on_device(features, geometry, decoder, teacher, images, send_index, tile_lists, tile_lengths):
    count = features.shape[0]
    tiles = tile_lists.shape[1]
    quarter = count // X
    basis, moments = pixel_tables(tiles)
    tables = order_tables()
    scale = 1.0 / math.sqrt(lax.axis_size("gs") * lax.axis_size("view") * tiles * PIX)
    vmem = pl.BlockSpec(memory_space=pltpu.VMEM)
    hbm = pl.BlockSpec(memory_space=pl.ANY)
    tile = (8, 128)
    inputs = (
        send_index[0], features, geometry.reshape(9, 1, count), decoder, images.reshape(3, 1, tiles * PIX),
        tile_lists[0], tile_lengths, teacher[0], jnp.asarray(basis), jnp.asarray(moments), jnp.asarray(tables),
    )
    feature_grad, geo_own, decoder_grad = pl.pallas_call(
        functools.partial(step_kernel, scale),
        in_specs=[hbm] * len(inputs),
        out_specs=[vmem] * 3,
        out_shape=[
            jax.ShapeDtypeStruct((quarter, FEAT), F32),
            jax.ShapeDtypeStruct((9, 1, count), F32),
            jax.ShapeDtypeStruct((FEAT, CT), F32),
        ],
        scratch_shapes=[
            *(pltpu.VMEM(array.shape, array.dtype) for array in inputs),
            pltpu.SemaphoreType.DMA((len(inputs),)),
            pltpu.VMEM((count, count), BF16),
            pltpu.VMEM((128, count), BF16),
            pltpu.VMEM((128, count), F32),
            pltpu.VMEM((48, count), BF16),
            pltpu.VMEM((48, count), F32),
            *exchange_buffers(BF16),
            pltpu.VMEM((128, 128), F32),
            pltpu.VMEM((16, count), F32),
            pltpu.VMEM((16, count), F32),
            pltpu.VMEM((128, count), F32),
            pltpu.VMEM((count, 2 * FEAT), BF16),
            pltpu.VMEM((FEAT + 32, count), BF16),
            pltpu.VMEM((tiles, count, PIX), F32),
            pltpu.VMEM((tiles, count, PIX), F32),
            pltpu.VMEM((tiles, count, 2 * PIX), BF16),
            pltpu.VMEM((count, 2 * PIX), BF16),
            pltpu.VMEM((count, PIX), F32),
            pltpu.VMEM((count, PIX), F32),
            pltpu.VMEM((LIST, PIX), F32),
            pltpu.VMEM((LIST, PIX), F32),
            pltpu.VMEM((LIST, PIX), F32),
            pltpu.VMEM((tiles, LIST, LIST), F32),
            pltpu.VMEM((2 * FEAT, PIX), F32),
            pltpu.VMEM((tiles, 2 * FEAT, PIX), BF16),
            pltpu.VMEM((tiles, PIX, 2 * FEAT), BF16),
            pltpu.VMEM((count, 2 * FEAT), F32),
            pltpu.VMEM((FEAT, CT), F32),
            *exchange_buffers(F32),
            pltpu.VMEM((X * C, Z, *tile), F32),
            pltpu.VMEM((X * C, Z, *tile), F32),
            pltpu.VMEM((Z, *tile), F32),
            pltpu.VMEM((Z, *tile), F32),
            pltpu.VMEM(tile, F32),
            pltpu.VMEM((Y, *tile), F32),
            pltpu.VMEM(tile, F32),
            pltpu.VMEM((Z, *tile), F32),
            pltpu.VMEM((X * C, Z, *tile), F32),
            pltpu.SemaphoreType.DMA((5, 2, 8)),
            pltpu.VMEM((count, 2 * FEAT), BF16),
            pltpu.VMEM((X, quarter, FEAT), F32),
            pltpu.VMEM((X, quarter, FEAT), F32),
            pltpu.SemaphoreType.DMA((2, X)),
        ],
        compiler_params=pltpu.CompilerParams(collective_id=0, has_side_effects=True),
        name="step",
    )(*inputs)
    return (feature_grad, geo_own.reshape(1, 9, count), decoder_grad)


def solution(mesh):
    placed = (
        P("gs", None),
        P("view", None, "gs"),
        P(),
        P("view", "gs", None),
        P("view", None, "gs"),
        P("view", "gs", None),
        P("view", "gs", None),
        P("view", "gs"),
    )
    return jax.shard_map(
        on_device,
        mesh=mesh,
        in_specs=placed,
        out_specs=(P(("gs", "view"), None), P("view", None, "gs"), P()),
        check_vma=False,
    )
```
